256 devices in a mesh: sta: 64 (over x_lo, z, y), tpl: 4 (over x_hi, core).
Axes of the slice: x: 4 (x_hi: 2, x_lo: 2; x = x_hi * 2 + x_lo), y: 4, z: 8, core: 2. Of those that a mesh axis runs over, the one named last changes fastest.
Arguments:
- waveform: float32 [128, 1536], P('sta', 'tpl'), may hold values from -6 to 6
- fir_taps: float32 [64], replicated, may hold values from -0.75 to 0.75
- templates: bfloat16 [512, 128, 1024], P('tpl', 'sta'), may hold values from -6 to 6
- presence: int32 [512, 128], P('tpl', 'sta'), may hold values from 0 to 1
- moveout: int32 [512, 128], P('tpl', 'sta'), may hold values from 0 to 128
Outputs:
- network_stack: float32 [4, 128, 384], P('tpl', 'sta')
The draws below stay inside these ranges and needn't reach their ends.
All inputs are finite; a program needn't handle non-finite values.
Results may differ from the reference program's by a relative error of at most 0.0029.
Values may be sent and summed in bfloat16 or wider, within the bound.
A program may use at most 64 MiB of HBM per device.

```python
import jax
import jax.numpy as jnp
from jax import lax

TPL = 512
L = 1024
TAPS = 64
BLK = 128
SHIFT_MOST = 128
STA = 128
NS = 1536
TPL_BLOCK = 128
GROUPS = 4


def draw_presence(key, part):
    key_rate, key_bits = jax.random.split(key)
    levels = jax.random.randint(key_rate, (TPL, 1), 2, 10)
    coin_flips = jax.random.randint(key_bits, (TPL, STA), 0, 10)
    return (coin_flips < levels).astype(jnp.int32)


def with_ends(array, key, least, high):
    shape = array.shape
    index_at = [jax.random.randint(jax.random.fold_in(key, axis), (), 0, shape[axis]) for axis in range(len(shape))]
    array = array.at[tuple(index_at)].set(least)
    longest = shape.index(max(shape))
    index_at[longest] = (index_at[longest] + 1) % shape[longest]
    return array.at[tuple(index_at)].set(high)


def level_of(own_key, shape, shards, low, high):
    loudness, own = 1.0, jax.random.fold_in(own_key, 6)
    for dim, parts in shards:
        steps = jnp.exp(jax.random.uniform(jax.random.fold_in(own, dim), (parts,), jnp.float32, low / len(shards), high / len(shards)))
        loudness = loudness * jnp.repeat(steps, shape[dim] // parts).reshape([-1 if axis == dim else 1 for axis in range(len(shape))])
    return loudness


def centred(stream_key, extent, deviation, bound, cuts=(), held_as=jnp.bfloat16):
    values = jax.random.normal(stream_key, extent, jnp.float32) * deviation
    if len(cuts) > 0:
        values = level_of(stream_key, extent, cuts, -0.22, 0.18) * values
    return jnp.clip(values, min=-bound, max=bound).astype(held_as)


def setup_inputs(seed: int = 0) -> dict:
    keys = jax.random.split(jax.random.key(seed), 6)
    return {
        "waveform": centred(keys[0], (STA, NS), 1.0, 6.0, ((0, 64), (1, 4)), jnp.float32),
        "fir_taps": centred(keys[1], (TAPS,), TAPS ** -0.5, 0.75, (), jnp.float32),
        "templates": centred(keys[2], (TPL, STA, L), 1.0, 6.0, ((0, 4), (1, 64))),
        "presence": draw_presence(jax.random.fold_in(keys[5], 71), 0),
        "moveout": with_ends(jax.random.randint(keys[4], (TPL, STA), 0, SHIFT_MOST + 1), jax.random.fold_in(keys[4], 1), 0, SHIFT_MOST).astype(jnp.int32),
    }


epsilon = 1e-06

def fir_apply(extended, coeffs):
    result = lax.conv_general_dilated(extended[:, None, :], coeffs[::-1][None, None, :], (1,), 'VALID', precision=lax.Precision.HIGHEST)
    return result[:, 0, :]

def hankel(samples):
    leading = samples.shape[:-1]
    row_total = samples.shape[-1] // BLK
    row_blocks = samples.reshape(leading + (row_total, BLK))
    windows = jnp.concatenate([row_blocks[..., :-1, :], row_blocks[..., 1:, :]], axis=-1)
    tiled_win = jnp.tile(windows, (1,) * (windows.ndim - 1) + (BLK + 1,))
    flat_win = tiled_win[..., :BLK * (2 * BLK + 1)]
    return flat_win.reshape(windows.shape[:-1] + (BLK, 2 * BLK + 1))[..., :BLK]

def reference(waveform, fir_taps, templates, presence, moveout):
    extended = jnp.pad(waveform, ((0, 0), (TAPS - 1, 0)))
    filtered = fir_apply(extended, fir_taps).astype(jnp.bfloat16)
    corr_len = NS - L
    out_len = corr_len - SHIFT_MOST
    time_blocks = corr_len // BLK
    values = filtered.astype(jnp.float32)
    prefix = jnp.concatenate([jnp.zeros((STA, 1), jnp.float32), jnp.cumsum(values * values, axis=1)], axis=1)
    energy = prefix[:, L:L + corr_len] - prefix[:, :corr_len]

    def station(stack_sum, station_id):
        series = lax.dynamic_index_in_dim(filtered, station_id, 0, keepdims=False)
        hankel_rows = hankel(series).astype(jnp.float32)
        templ_rows = lax.dynamic_index_in_dim(templates, station_id, 1, keepdims=False)
        templ_split = templ_rows.astype(jnp.float32).reshape(TPL, L // BLK, BLK)
        products = jnp.zeros((TPL, time_blocks, BLK), jnp.float32)
        for offset in range(L // BLK):
            products = products + jnp.einsum('kb,cbd->kcd', templ_split[:, offset], hankel_rows[offset:offset + time_blocks], precision=lax.Precision.HIGHEST)
        products = products.reshape(TPL, corr_len)
        templ_norm = jnp.sqrt(lax.optimization_barrier(jnp.sum(templ_rows.astype(jnp.float32) ** 2, axis=-1)) + epsilon)
        station_energy = lax.dynamic_index_in_dim(energy, station_id, 0, keepdims=False)
        correlation = products / (templ_norm[:, None] * jnp.sqrt(station_energy)[None, :])
        shifts = lax.dynamic_index_in_dim(moveout, station_id, 1, keepdims=False).astype(jnp.int32)
        weights = lax.dynamic_index_in_dim(presence, station_id, 1, keepdims=False).astype(jnp.float32)
        aligned = jax.vmap(lambda series_row, offset_value: lax.dynamic_slice_in_dim(series_row, offset_value, out_len))(correlation, shifts)
        return (stack_sum + weights[:, None] * aligned, None)
    stack_sum, _ = lax.scan(station, jnp.zeros((TPL, out_len), jnp.float32), jnp.arange(STA, dtype=jnp.int32))
    return stack_sum.reshape(GROUPS, TPL_BLOCK, out_len)
```

```python
import functools

import jax
import jax.numpy as jnp
from jax import lax
from jax.experimental import pallas as pl
from jax.experimental.pallas import tpu as pltpu
from jax.sharding import PartitionSpec as P

BLK = 128
SHIFT_MOST = 128
EPSILON = 1e-06
MESH = pl.DeviceIdType.MESH


def lane_gather(values, index):
    return jnp.take_along_axis(values, index, axis=1, mode="promise_in_bounds")


def sta_offsets(n_sta):
    dims = (2, 8, 4) if n_sta == 64 else (1, n_sta, 1)
    steps = [
        (dx, dz, dy) for dx in range(dims[0]) for dz in range(dims[1]) for dy in range(dims[2])
    ][1:]

    def hops(step):
        return sum(min(d, n - d) for d, n in zip(step, dims))

    return dims, sorted(steps, key=lambda step: -hops(step))


def peer(me, step, dims):
    x, rest = me // (dims[1] * dims[2]), me % (dims[1] * dims[2])
    z, y = rest // dims[2], rest % dims[2]
    x = (x + step[0]) % dims[0]
    z = (z + step[1]) % dims[1]
    y = (y + step[2]) % dims[2]
    return (x * dims[1] + z) * dims[2] + y


def kernel(
    n_sta,
    n_tpl,
    wave_ref,
    fir_ref,
    tpl_ref,
    pres_ref,
    mov_ref,
    out_ref,
    wave_buf,
    tpl_raw,
    rows32,
    tpl_split,
    send_buf,
    recv_buf,
    local_sem,
    wave_send,
    wave_recv,
    stack_send,
    stack_recv,
):
    me_s, me_t = lax.axis_index("sta"), lax.axis_index("tpl")
    dims, steps = sta_offsets(n_sta)
    stations = wave_ref.shape[0]
    n_rows = tpl_ref.shape[0]
    lag_blocks = tpl_ref.shape[2] // BLK
    own_rows = n_rows // n_sta
    seg_blocks = wave_ref.shape[1] // BLK
    wave_blocks = seg_blocks * n_tpl
    time_blocks = wave_blocks - lag_blocks
    out_blocks = time_blocks - 1

    barrier = pltpu.get_barrier_semaphore()
    for step in range(1, n_tpl):
        pl.semaphore_signal(barrier, inc=1, device_id={"tpl": lax.rem(me_t + step, n_tpl)}, device_id_type=MESH)
    for step in steps:
        pl.semaphore_signal(barrier, inc=1, device_id={"sta": peer(me_s, step, dims)}, device_id_type=MESH)

    own_wave = pltpu.make_async_copy(wave_ref, wave_buf.at[me_t], local_sem.at[0])
    own_wave.start()
    tpl_copies = []
    for b in range(lag_blocks):
        tpl_copies.append(
            pltpu.make_async_copy(
                tpl_ref.at[:, :, pl.ds(b * BLK, BLK)], tpl_raw.at[b], local_sem.at[1 + b]
            )
        )
        tpl_copies[-1].start()

    row_view = tpl_raw.reshape(lag_blocks, n_rows * stations, BLK)
    squares = [jnp.zeros((n_rows, BLK), jnp.float32) for _ in range(stations)]
    for b in range(lag_blocks):
        tpl_copies[b].wait()
        rows32[b % 2] = row_view[b].astype(jnp.float32)
        for s in range(stations):
            part = rows32[b % 2, pl.ds(s, n_rows, stride=stations), :]
            squares[s] = squares[s] + part * part
            tpl_split[s, lag_blocks // 2 - 1 - b // 2, :, (b % 2) * BLK : (b % 2 + 1) * BLK] = part.astype(
                jnp.bfloat16
            )

    lane = lax.broadcasted_iota(jnp.int32, (n_rows, BLK), 1)
    weights, gather_at, first_block = [], [], []
    for s in range(stations):
        norm = jnp.sqrt(jnp.sum(squares[s], axis=1, keepdims=True) + EPSILON)
        moved = jnp.transpose(jnp.broadcast_to(mov_ref[s : s + 1, :], (BLK, n_rows)))
        present = jnp.transpose(jnp.broadcast_to(pres_ref[s : s + 1, :].astype(jnp.float32), (BLK, n_rows)))
        weights.append(present / norm)
        position = lane + moved
        gather_at.append(position & (BLK - 1))
        first_block.append(position < BLK)

    pl.semaphore_wait(barrier, n_tpl - 1 + len(steps))
    wave_copies = []
    for step in range(1, n_tpl):
        wave_copies.append(
            pltpu.make_async_remote_copy(
                src_ref=wave_ref,
                dst_ref=wave_buf.at[me_t],
                send_sem=wave_send.at[step - 1],
                recv_sem=wave_recv.at[step - 1],
                device_id={"tpl": lax.rem(me_t + step, n_tpl)},
                device_id_type=MESH,
            )
        )
        wave_copies[-1].start()
    own_wave.wait()
    for copy in wave_copies:
        copy.wait()

    pieces = [
        wave_buf[c // seg_blocks, :, (c % seg_blocks) * BLK : (c % seg_blocks + 1) * BLK] for c in range(wave_blocks)
    ]
    now = jnp.concatenate(pieces, axis=0)
    before = jnp.concatenate([jnp.zeros((stations, BLK), jnp.float32)] + pieces[:-1], axis=0)
    row_lane = lax.broadcasted_iota(jnp.int32, now.shape, 1)
    sums = [now * fir_ref[0, 0], None]
    for i in range(1, fir_ref.shape[1]):
        term = pltpu.roll(jnp.where(row_lane < BLK - i, now, before), i, 1) * fir_ref[0, i]
        sums[i % 2] = term if sums[i % 2] is None else sums[i % 2] + term
    filtered = (sums[0] + sums[1]).astype(jnp.bfloat16).astype(jnp.float32)

    power = filtered * filtered
    after = power
    upto = power
    shift = 1
    while shift < BLK:
        after = after + jnp.where(row_lane < BLK - shift, pltpu.roll(after, BLK - shift, 1), 0.0)
        upto = upto + jnp.where(row_lane >= shift, pltpu.roll(upto, shift, 1), 0.0)
        shift *= 2
    upto = jnp.where(row_lane >= 1, pltpu.roll(upto, 1, 1), 0.0)
    total = jnp.sum(power, axis=1, keepdims=True)
    span = stations * time_blocks
    energy = after[:span] + upto[stations * lag_blocks :]
    for b in range(1, lag_blocks):
        energy = energy + total[stations * b : stations * b + span]
    inverse = 1.0 / jnp.sqrt(energy)

    hankel_at = lax.broadcasted_iota(jnp.int32, (BLK, BLK), 0) + lax.broadcasted_iota(jnp.int32, (BLK, BLK), 1)
    hankel_index = hankel_at & (BLK - 1)
    hankel_first = hankel_at < BLK
    stack = [None] * out_blocks
    for s in range(stations):
        turned = [
            lane_gather(
                jnp.broadcast_to(filtered[stations * c + s : stations * c + s + 1, :], (BLK, BLK)), hankel_index
            )
            for c in range(wave_blocks)
        ]
        blocks = [
            jnp.where(hankel_first, turned[c], turned[c + 1]).astype(jnp.bfloat16) for c in range(wave_blocks - 1)
        ]
        pairs = lag_blocks // 2
        time_pairs = time_blocks // 2
        raw = [None] * time_pairs
        for c in range(pairs + time_pairs - 1):
            tile = jnp.concatenate(
                [
                    jnp.concatenate([blocks[2 * c], blocks[2 * c + 1]], axis=1),
                    jnp.concatenate([blocks[2 * c + 1], blocks[2 * c + 2]], axis=1),
                ],
                axis=0,
            )
            used = [p for p in range(time_pairs) if 0 <= c - p < pairs]
            first = pairs - 1 - (c - used[0])
            rows = tpl_split[s, first : first + len(used)].reshape(len(used) * n_rows, 2 * BLK)
            product = jnp.dot(rows, tile, preferred_element_type=jnp.float32)
            for i, p in enumerate(used):
                part = product[i * n_rows : (i + 1) * n_rows]
                raw[p] = part if raw[p] is None else raw[p] + part
        moved = []
        for b in range(time_blocks):
            scaled = raw[b // 2][:, (b % 2) * BLK : (b % 2 + 1) * BLK] * inverse[stations * b + s : stations * b + s + 1]
            moved.append(lane_gather(scaled, gather_at[s]))
        for b in range(out_blocks):
            term = weights[s] * jnp.where(first_block[s], moved[b], moved[b + 1])
            stack[b] = term if stack[b] is None else stack[b] + term
    send_buf[...] = jnp.concatenate(stack, axis=1).astype(jnp.bfloat16).reshape(send_buf.shape)

    for slot, step in enumerate(steps):
        to = peer(me_s, step, dims)
        pltpu.make_async_remote_copy(
            src_ref=send_buf.at[to],
            dst_ref=recv_buf.at[slot],
            send_sem=stack_send,
            recv_sem=stack_recv,
            device_id={"sta": to},
            device_id_type=MESH,
        ).start()
    own = send_buf[me_s].astype(jnp.float32)
    arrived = recv_buf.at[pl.ds(0, len(steps))]
    pltpu.make_async_copy(arrived, arrived, stack_recv).wait()
    out_ref[0] = own + jnp.sum(arrived[...].astype(jnp.float32), axis=0)
    pltpu.make_async_copy(arrived, arrived, stack_send).wait()


def shards(n_sta, n_tpl, waveform, fir_taps, templates, presence, moveout):
    stations, segment = waveform.shape
    n_rows, _, lags = templates.shape
    own_rows = n_rows // n_sta
    out_len = segment * n_tpl - lags - SHIFT_MOST
    lag_blocks = lags // BLK
    hbm = pl.BlockSpec(memory_space=pl.ANY)
    vmem = pl.BlockSpec(memory_space=pltpu.VMEM)
    return pl.pallas_call(
        functools.partial(kernel, n_sta, n_tpl),
        out_shape=jax.ShapeDtypeStruct((1, own_rows, out_len), jnp.float32),
        in_specs=[hbm, pl.BlockSpec(memory_space=pltpu.SMEM), hbm, vmem, vmem],
        out_specs=vmem,
        scratch_shapes=[
            pltpu.VMEM((n_tpl, stations, segment), jnp.float32),
            pltpu.VMEM((lag_blocks, n_rows, stations, BLK), jnp.bfloat16),
            pltpu.VMEM((2, n_rows * stations, BLK), jnp.float32),
            pltpu.VMEM((stations, lag_blocks // 2, n_rows, 2 * BLK), jnp.bfloat16),
            pltpu.VMEM((n_sta, own_rows, out_len), jnp.bfloat16),
            pltpu.VMEM((n_sta, own_rows, out_len), jnp.bfloat16),
            pltpu.SemaphoreType.DMA((1 + lag_blocks,)),
            pltpu.SemaphoreType.DMA((n_tpl - 1,)),
            pltpu.SemaphoreType.DMA((n_tpl - 1,)),
            pltpu.SemaphoreType.DMA,
            pltpu.SemaphoreType.DMA,
        ],
        compiler_params=pltpu.CompilerParams(collective_id=0, has_side_effects=True),
    )(waveform, fir_taps[None, :], templates, presence.T, moveout.T)


def solution(mesh):
    placed = (P("sta", "tpl"), P(), P("tpl", "sta", None), P("tpl", "sta"), P("tpl", "sta"))
    return jax.shard_map(
        functools.partial(shards, mesh.shape["sta"], mesh.shape["tpl"]),
        mesh=mesh,
        in_specs=placed,
        out_specs=P("tpl", "sta", None),
        check_vma=False,
    )
```

```python
import functools

import jax
import jax.numpy as jnp
from jax import lax
from jax.experimental import pallas as pl
from jax.experimental.pallas import tpu as pltpu
from jax.sharding import PartitionSpec as P

BLK = 128
SHIFT_MOST = 128
EPSILON = 1e-06
MESH = pl.DeviceIdType.MESH


def lane_gather(values, index):
    return jnp.take_along_axis(values, index, axis=1, mode="promise_in_bounds")


def sta_dims(n_sta):
    return {64: (2, 8, 4), 8: (2, 2, 2), 4: (2, 2, 1)}.get(n_sta, (1, n_sta, 1))


def sta_offsets(dims):
    steps = [(dx, dz, dy) for dx in range(dims[0]) for dz in range(dims[1]) for dy in range(dims[2])][1:]
    return sorted(steps, key=lambda step: -sum(min(d, n - d) for d, n in zip(step, dims)))


def peer(me, step, dims):
    x, rest = me // (dims[1] * dims[2]), me % (dims[1] * dims[2])
    z, y = rest // dims[2], rest % dims[2]
    x = (x + step[0]) % dims[0]
    z = (z + step[1]) % dims[1]
    y = (y + step[2]) % dims[2]
    return (x * dims[1] + z) * dims[2] + y


def kernel(
    n_sta,
    n_tpl,
    wave_ref,
    fir_hbm,
    tpl_ref,
    pres_hbm,
    mov_hbm,
    out_ref,
    wave_buf,
    tpl_raw,
    rows32,
    tpl_split,
    send_buf,
    recv_buf,
    fir_ref,
    pres_ref,
    mov_ref,
    local_sem,
    small_sem,
    chain_sem,
    wave_send,
    wave_recv,
    stack_send,
    stack_recv,
):
    me_s, me_t = lax.axis_index("sta"), lax.axis_index("tpl")
    dims = sta_dims(n_sta)
    steps = sta_offsets(dims)
    stations = wave_ref.shape[0]
    n_rows = tpl_ref.shape[0]
    lag_blocks = tpl_ref.shape[2] // BLK
    own_rows = n_rows // n_sta
    seg_blocks = wave_ref.shape[1] // BLK
    wave_blocks = seg_blocks * n_tpl
    time_blocks = wave_blocks - lag_blocks
    out_blocks = time_blocks - 1

    near_z = [(0, dz, 0) for dz in range(1, dims[1]) if min(dz, dims[1] - dz) <= 2]
    all_y = [(0, 0, dy) for dy in range(1, dims[2])]
    all_x = [(dx, 0, 0) for dx in range(1, dims[0])]

    def tell(sem, steps):
        for step in steps:
            pl.semaphore_signal(sem, inc=1, device_id={"sta": peer(me_s, step, dims)}, device_id_type=MESH)

    def hear(sem, steps):
        if steps:
            pl.semaphore_wait(sem, len(steps))

    barrier = pltpu.get_barrier_semaphore()
    for step in range(n_tpl - 1, 0, -1):
        pl.semaphore_signal(barrier, inc=1, device_id={"tpl": lax.rem(me_t + step, n_tpl)}, device_id_type=MESH)
    tell(barrier, all_x + all_y + near_z)

    own_wave = pltpu.make_async_copy(wave_ref, wave_buf.at[me_t], local_sem.at[0])
    own_wave.start()
    small_copies = [
        pltpu.make_async_copy(mov_hbm, mov_ref, small_sem.at[0]),
        pltpu.make_async_copy(pres_hbm, pres_ref, small_sem.at[1]),
        pltpu.make_async_copy(fir_hbm, fir_ref, small_sem.at[2]),
    ]
    for copy in small_copies:
        copy.start()
    tpl_copies = []
    for b in range(lag_blocks):
        tpl_copies.append(
            pltpu.make_async_copy(
                tpl_ref.at[:, :, pl.ds(b * BLK, BLK)], tpl_raw.at[b], local_sem.at[1 + b]
            )
        )
        tpl_copies[-1].start()

    pl.semaphore_wait(barrier, n_tpl - 1 + len(all_x + all_y + near_z))
    wave_copies = []
    for step in range(1, n_tpl):
        wave_copies.append(
            pltpu.make_async_remote_copy(
                src_ref=wave_ref,
                dst_ref=wave_buf.at[me_t],
                send_sem=wave_send.at[step - 1],
                recv_sem=wave_recv.at[step - 1],
                device_id={"tpl": lax.rem(me_t + step, n_tpl)},
                device_id_type=MESH,
            )
        )
        wave_copies[-1].start()
    tell(chain_sem.at[0], near_z)

    row_view = tpl_raw.reshape(lag_blocks, n_rows * stations, BLK)
    squares = [jnp.zeros((n_rows, BLK), jnp.float32) for _ in range(stations)]
    for b in range(lag_blocks):
        tpl_copies[b].wait()
        rows32[b % 2] = row_view[b].astype(jnp.float32)
        for s in range(stations):
            part = rows32[b % 2, pl.ds(s, n_rows, stride=stations), :]
            squares[s] = squares[s] + part * part
            tpl_split[s, lag_blocks // 2 - 1 - b // 2, :, (b % 2) * BLK : (b % 2 + 1) * BLK] = part.astype(
                jnp.bfloat16
            )

    hear(chain_sem.at[0], near_z)
    tell(chain_sem.at[1], all_y)
    for copy in small_copies:
        copy.wait()
    lane = lax.broadcasted_iota(jnp.int32, (n_rows, BLK), 1)
    weights, gather_at, first_block = [], [], []
    for s in range(stations):
        norm = jnp.sqrt(jnp.sum(squares[s], axis=1, keepdims=True) + EPSILON)
        moved = jnp.transpose(jnp.broadcast_to(mov_ref[s : s + 1, :], (BLK, n_rows)))
        present = jnp.transpose(jnp.broadcast_to(pres_ref[s : s + 1, :].astype(jnp.float32), (BLK, n_rows)))
        weights.append(present / norm)
        position = lane + moved
        gather_at.append(position & (BLK - 1))
        first_block.append(position < BLK)

    own_wave.wait()
    for copy in wave_copies:
        copy.wait()

    pieces = [
        wave_buf[c // seg_blocks, :, (c % seg_blocks) * BLK : (c % seg_blocks + 1) * BLK] for c in range(wave_blocks)
    ]
    now = jnp.concatenate(pieces, axis=0)
    before = jnp.concatenate([jnp.zeros((stations, BLK), jnp.float32)] + pieces[:-1], axis=0)
    row_lane = lax.broadcasted_iota(jnp.int32, now.shape, 1)
    sums = [now * fir_ref[0, 0], None]
    for i in range(1, fir_ref.shape[1]):
        term = pltpu.roll(jnp.where(row_lane < BLK - i, now, before), i, 1) * fir_ref[0, i]
        sums[i % 2] = term if sums[i % 2] is None else sums[i % 2] + term
    filtered = (sums[0] + sums[1]).astype(jnp.bfloat16).astype(jnp.float32)

    hear(chain_sem.at[1], all_y)
    tell(chain_sem.at[2], all_x)

    power = filtered * filtered
    high = power.astype(jnp.bfloat16)
    low = (power - high.astype(jnp.float32)).astype(jnp.bfloat16)
    taken = lax.broadcasted_iota(jnp.int32, (BLK, BLK), 0)
    at = lax.broadcasted_iota(jnp.int32, (BLK, BLK), 1)
    rest = jnp.where(taken >= at, 1.0, 0.0)
    masks = jnp.concatenate([rest, 1.0 - rest, jnp.ones((BLK, BLK), jnp.float32)], axis=1)
    sums = jnp.dot(
        jnp.concatenate([high, low], axis=0), masks.astype(jnp.bfloat16), preferred_element_type=jnp.float32
    )
    sums = sums[: power.shape[0]] + sums[power.shape[0] :]
    span = stations * time_blocks
    energy = sums[:span, :BLK] + sums[stations * lag_blocks :, BLK : 2 * BLK]
    for b in range(1, lag_blocks):
        energy = energy + sums[stations * b : stations * b + span, 2 * BLK :]
    inverse = 1.0 / jnp.sqrt(energy)

    hankel_at = lax.broadcasted_iota(jnp.int32, (BLK, BLK), 0) + lax.broadcasted_iota(jnp.int32, (BLK, BLK), 1)
    hankel_index = hankel_at & (BLK - 1)
    hankel_first = hankel_at < BLK
    stack = [None] * out_blocks
    for s in range(stations):
        turned = [
            lane_gather(
                jnp.broadcast_to(filtered[stations * c + s : stations * c + s + 1, :], (BLK, BLK)), hankel_index
            )
            for c in range(wave_blocks)
        ]
        blocks = [
            jnp.where(hankel_first, turned[c], turned[c + 1]).astype(jnp.bfloat16) for c in range(wave_blocks - 1)
        ]
        pairs = lag_blocks // 2
        time_pairs = time_blocks // 2
        raw = [None] * time_pairs
        for c in range(pairs + time_pairs - 1):
            tile = jnp.concatenate(
                [
                    jnp.concatenate([blocks[2 * c], blocks[2 * c + 1]], axis=1),
                    jnp.concatenate([blocks[2 * c + 1], blocks[2 * c + 2]], axis=1),
                ],
                axis=0,
            )
            used = [p for p in range(time_pairs) if 0 <= c - p < pairs]
            first = pairs - 1 - (c - used[0])
            rows = tpl_split[s, first : first + len(used)].reshape(len(used) * n_rows, 2 * BLK)
            product = jnp.dot(rows, tile, preferred_element_type=jnp.float32)
            for i, p in enumerate(used):
                part = product[i * n_rows : (i + 1) * n_rows]
                raw[p] = part if raw[p] is None else raw[p] + part
        moved = []
        for b in range(time_blocks):
            scaled = raw[b // 2][:, (b % 2) * BLK : (b % 2 + 1) * BLK] * inverse[stations * b + s : stations * b + s + 1]
            moved.append(lane_gather(scaled, gather_at[s]))
        for b in range(out_blocks):
            term = weights[s] * jnp.where(first_block[s], moved[b], moved[b + 1])
            stack[b] = term if stack[b] is None else stack[b] + term
    send_buf[...] = jnp.concatenate(stack, axis=1).astype(jnp.bfloat16).reshape(send_buf.shape)

    hear(chain_sem.at[2], all_x)
    for slot, step in enumerate(steps):
        to = peer(me_s, step, dims)
        pltpu.make_async_remote_copy(
            src_ref=send_buf.at[to],
            dst_ref=recv_buf.at[slot],
            send_sem=stack_send,
            recv_sem=stack_recv,
            device_id={"sta": to},
            device_id_type=MESH,
        ).start()
    own = send_buf[me_s].astype(jnp.float32)
    arrived = recv_buf.at[pl.ds(0, len(steps))]
    pltpu.make_async_copy(arrived, arrived, stack_recv).wait()
    out_ref[0] = own + jnp.sum(arrived[...].astype(jnp.float32), axis=0)
    pltpu.make_async_copy(arrived, arrived, stack_send).wait()


def shards(n_sta, n_tpl, waveform, fir_taps, templates, presence, moveout):
    stations, segment = waveform.shape
    n_rows, _, lags = templates.shape
    own_rows = n_rows // n_sta
    out_len = segment * n_tpl - lags - SHIFT_MOST
    lag_blocks = lags // BLK
    hbm = pl.BlockSpec(memory_space=pl.ANY)
    vmem = pl.BlockSpec(memory_space=pltpu.VMEM)
    return pl.pallas_call(
        functools.partial(kernel, n_sta, n_tpl),
        out_shape=pltpu.VMEM((1, own_rows, out_len), jnp.float32),
        in_specs=[hbm] * 5,
        out_specs=vmem,
        scratch_shapes=[
            pltpu.VMEM((n_tpl, stations, segment), jnp.float32),
            pltpu.VMEM((lag_blocks, n_rows, stations, BLK), jnp.bfloat16),
            pltpu.VMEM((2, n_rows * stations, BLK), jnp.float32),
            pltpu.VMEM((stations, lag_blocks // 2, n_rows, 2 * BLK), jnp.bfloat16),
            pltpu.VMEM((n_sta, own_rows, out_len), jnp.bfloat16),
            pltpu.VMEM((n_sta, own_rows, out_len), jnp.bfloat16),
            pltpu.SMEM((1, fir_taps.shape[0]), jnp.float32),
            pltpu.VMEM((stations, n_rows), jnp.int32),
            pltpu.VMEM((stations, n_rows), jnp.int32),
            pltpu.SemaphoreType.DMA((1 + lag_blocks,)),
            pltpu.SemaphoreType.DMA((3,)),
            pltpu.SemaphoreType.REGULAR((3,)),
            pltpu.SemaphoreType.DMA((n_tpl - 1,)),
            pltpu.SemaphoreType.DMA((n_tpl - 1,)),
            pltpu.SemaphoreType.DMA,
            pltpu.SemaphoreType.DMA,
        ],
        compiler_params=pltpu.CompilerParams(collective_id=0, has_side_effects=True),
    )(waveform, fir_taps[None, :], templates, presence.T, moveout.T)


def solution(mesh):
    placed = (P("sta", "tpl"), P(), P("tpl", "sta", None), P("tpl", "sta"), P("tpl", "sta"))
    return jax.shard_map(
        functools.partial(shards, mesh.shape["sta"], mesh.shape["tpl"]),
        mesh=mesh,
        in_specs=placed,
        out_specs=P("tpl", "sta", None),
        check_vma=False,
    )
```

```python
import functools

import jax
import jax.numpy as jnp
from jax import lax
from jax.experimental import pallas as pl
from jax.experimental.pallas import tpu as pltpu
from jax.sharding import PartitionSpec as P

BLK = 128
SHIFT_MOST = 128
EPSILON = 1e-06
MESH = pl.DeviceIdType.MESH


def lane_gather(values, index):
    return jnp.take_along_axis(values, index, axis=1, mode="promise_in_bounds")


def sta_dims(n_sta):
    return {64: (2, 8, 4), 8: (2, 2, 2), 4: (2, 2, 1)}.get(n_sta, (1, n_sta, 1))


def sta_offsets(dims):
    steps = [(dx, dz, dy) for dx in range(dims[0]) for dz in range(dims[1]) for dy in range(dims[2])][1:]
    return sorted(steps, key=lambda step: -sum(min(d, n - d) for d, n in zip(step, dims)))


def peer(me, step, dims):
    x, rest = me // (dims[1] * dims[2]), me % (dims[1] * dims[2])
    z, y = rest // dims[2], rest % dims[2]
    x = (x + step[0]) % dims[0]
    z = (z + step[1]) % dims[1]
    y = (y + step[2]) % dims[2]
    return (x * dims[1] + z) * dims[2] + y


def kernel(
    n_sta,
    n_tpl,
    wave_ref,
    fir_hbm,
    tpl_ref,
    pres_hbm,
    mov_hbm,
    out_ref,
    wave_buf,
    tpl_raw,
    rows32,
    tpl_split,
    send_buf,
    recv_buf,
    fir_ref,
    pres_ref,
    mov_ref,
    local_sem,
    small_sem,
    chain_sem,
    wave_send,
    wave_recv,
    stack_send,
    stack_recv,
):
    me_s, me_t = lax.axis_index("sta"), lax.axis_index("tpl")
    dims = sta_dims(n_sta)
    steps = sta_offsets(dims)
    stations = wave_ref.shape[0]
    n_rows = tpl_ref.shape[0]
    lag_blocks = tpl_ref.shape[2] // BLK
    own_rows = n_rows // n_sta
    seg_blocks = wave_ref.shape[1] // BLK
    wave_blocks = seg_blocks * n_tpl
    time_blocks = wave_blocks - lag_blocks
    out_blocks = time_blocks - 1

    def ring(axis, distance):
        hops = {distance % dims[axis], -distance % dims[axis]} - {0}
        return [tuple(hop if i == axis else 0 for i in range(3)) for hop in sorted(hops)]

    near = ring(0, 1) + ring(2, 1) + ring(1, 1)
    chain = [ring(1, 1), ring(1, 2), ring(2, 1), ring(2, 1), ring(0, 1)]

    def tell(sem, steps):
        for step in steps:
            pl.semaphore_signal(sem, inc=1, device_id={"sta": peer(me_s, step, dims)}, device_id_type=MESH)

    def hear(stage):
        if chain[stage]:
            pl.semaphore_wait(chain_sem.at[stage], len(chain[stage]))
        if stage + 1 < len(chain):
            tell(chain_sem.at[stage + 1], chain[stage + 1])

    barrier = pltpu.get_barrier_semaphore()
    for step in range(n_tpl - 1, 0, -1):
        pl.semaphore_signal(barrier, inc=1, device_id={"tpl": lax.rem(me_t + step, n_tpl)}, device_id_type=MESH)
    tell(barrier, near)

    own_wave = pltpu.make_async_copy(wave_ref, wave_buf.at[me_t], local_sem.at[0])
    own_wave.start()
    small_copies = [
        pltpu.make_async_copy(mov_hbm, mov_ref, small_sem.at[0]),
        pltpu.make_async_copy(pres_hbm, pres_ref, small_sem.at[1]),
        pltpu.make_async_copy(fir_hbm, fir_ref, small_sem.at[2]),
    ]
    for copy in small_copies:
        copy.start()
    tpl_copies = []
    for b in range(lag_blocks):
        tpl_copies.append(
            pltpu.make_async_copy(
                tpl_ref.at[:, :, pl.ds(b * BLK, BLK)], tpl_raw.at[b], local_sem.at[1 + b]
            )
        )
        tpl_copies[-1].start()

    pl.semaphore_wait(barrier, n_tpl - 1 + len(near))
    own_wave.wait()
    wave_copies = []
    for step in range(1, n_tpl):
        wave_copies.append(
            pltpu.make_async_remote_copy(
                src_ref=wave_buf.at[me_t],
                dst_ref=wave_buf.at[me_t],
                send_sem=wave_send.at[step - 1],
                recv_sem=wave_recv.at[step - 1],
                device_id={"tpl": lax.rem(me_t + step, n_tpl)},
                device_id_type=MESH,
            )
        )
        wave_copies[-1].start()
    tell(chain_sem.at[0], chain[0])

    row_view = tpl_raw.reshape(lag_blocks, n_rows * stations, BLK)
    squares = [jnp.zeros((n_rows, BLK), jnp.float32) for _ in range(stations)]
    for b in range(lag_blocks):
        if b == lag_blocks // 2:
            hear(0)
        tpl_copies[b].wait()
        rows32[b % 2] = row_view[b].astype(jnp.float32)
        for s in range(stations):
            part = rows32[b % 2, pl.ds(s, n_rows, stride=stations), :]
            squares[s] = squares[s] + part * part
            tpl_split[s, lag_blocks // 2 - 1 - b // 2, :, (b % 2) * BLK : (b % 2 + 1) * BLK] = part.astype(
                jnp.bfloat16
            )

    for copy in small_copies:
        copy.wait()
    lane = lax.broadcasted_iota(jnp.int32, (n_rows, BLK), 1)
    weights, gather_at, first_block = [], [], []
    for s in range(stations):
        norm = jnp.sqrt(jnp.sum(squares[s], axis=1, keepdims=True) + EPSILON)
        moved = jnp.transpose(jnp.broadcast_to(mov_ref[s : s + 1, :], (BLK, n_rows)))
        present = jnp.transpose(jnp.broadcast_to(pres_ref[s : s + 1, :].astype(jnp.float32), (BLK, n_rows)))
        weights.append(present / norm)
        position = lane + moved
        gather_at.append(position & (BLK - 1))
        first_block.append(position < BLK)

    hear(1)
    for copy in wave_copies:
        copy.wait()

    pieces = [
        wave_buf[c // seg_blocks, :, (c % seg_blocks) * BLK : (c % seg_blocks + 1) * BLK] for c in range(wave_blocks)
    ]
    now = jnp.concatenate(pieces, axis=0)
    before = jnp.concatenate([jnp.zeros((stations, BLK), jnp.float32)] + pieces[:-1], axis=0)
    row_lane = lax.broadcasted_iota(jnp.int32, now.shape, 1)
    sums = [now * fir_ref[0, 0], None]
    for i in range(1, fir_ref.shape[1]):
        term = pltpu.roll(jnp.where(row_lane < BLK - i, now, before), i, 1) * fir_ref[0, i]
        sums[i % 2] = term if sums[i % 2] is None else sums[i % 2] + term
    filtered = (sums[0] + sums[1]).astype(jnp.bfloat16).astype(jnp.float32)

    power = filtered * filtered
    high = power.astype(jnp.bfloat16)
    low = (power - high.astype(jnp.float32)).astype(jnp.bfloat16)
    taken = lax.broadcasted_iota(jnp.int32, (BLK, BLK), 0)
    at = lax.broadcasted_iota(jnp.int32, (BLK, BLK), 1)
    rest = jnp.where(taken >= at, 1.0, 0.0)
    masks = jnp.concatenate([rest, 1.0 - rest, jnp.ones((BLK, BLK), jnp.float32)], axis=1)
    sums = jnp.dot(
        jnp.concatenate([high, low], axis=0), masks.astype(jnp.bfloat16), preferred_element_type=jnp.float32
    )
    sums = sums[: power.shape[0]] + sums[power.shape[0] :]
    span = stations * time_blocks
    energy = sums[:span, :BLK] + sums[stations * lag_blocks :, BLK : 2 * BLK]
    for b in range(1, lag_blocks):
        energy = energy + sums[stations * b : stations * b + span, 2 * BLK :]
    inverse = 1.0 / jnp.sqrt(energy)

    tall = 16
    hankel_at = lax.broadcasted_iota(jnp.int32, (tall, BLK), 0) + lax.broadcasted_iota(jnp.int32, (tall, BLK), 1)
    hankel_index = hankel_at & (BLK - 1)
    hankel_first = hankel_at < BLK
    tall_lane = lax.broadcasted_iota(jnp.int32, (tall, BLK), 1)
    stack = [None] * out_blocks
    for s in range(stations):
        turned = [
            lane_gather(
                jnp.broadcast_to(filtered[stations * c + s : stations * c + s + 1, :], (tall, BLK)), hankel_index
            )
            for c in range(wave_blocks)
        ]
        heads = [
            jnp.where(hankel_first, turned[c], turned[min(c + 1, wave_blocks - 1)]).astype(jnp.bfloat16)
            for c in range(wave_blocks)
        ]
        blocks = [
            jnp.concatenate(
                [heads[c]]
                + [
                    pltpu.roll(jnp.where(tall_lane < q, heads[c + 1], heads[c]), BLK - q, 1)
                    for q in range(tall, BLK, tall)
                ],
                axis=0,
            )
            for c in range(wave_blocks - 1)
        ]
        pairs = lag_blocks // 2
        time_pairs = time_blocks // 2
        raw = [None] * time_pairs
        for c in range(pairs + time_pairs - 1):
            tile = jnp.concatenate(
                [
                    jnp.concatenate([blocks[2 * c], blocks[2 * c + 1]], axis=1),
                    jnp.concatenate([blocks[2 * c + 1], blocks[2 * c + 2]], axis=1),
                ],
                axis=0,
            )
            used = [p for p in range(time_pairs) if 0 <= c - p < pairs]
            first = pairs - 1 - (c - used[0])
            rows = tpl_split[s, first : first + len(used)].reshape(len(used) * n_rows, 2 * BLK)
            product = jnp.dot(rows, tile, preferred_element_type=jnp.float32)
            for i, p in enumerate(used):
                part = product[i * n_rows : (i + 1) * n_rows]
                raw[p] = part if raw[p] is None else raw[p] + part
        hear(2 + s) if stations == 2 else None
        moved = []
        for b in range(time_blocks):
            scaled = raw[b // 2][:, (b % 2) * BLK : (b % 2 + 1) * BLK] * inverse[stations * b + s : stations * b + s + 1]
            moved.append(lane_gather(scaled, gather_at[s]))
        for b in range(out_blocks):
            term = weights[s] * jnp.where(first_block[s], moved[b], moved[b + 1])
            stack[b] = term if stack[b] is None else stack[b] + term
    send_buf[...] = jnp.concatenate(stack, axis=1).astype(jnp.bfloat16).reshape(send_buf.shape)

    hear(4)
    for slot, step in enumerate(steps):
        to = peer(me_s, step, dims)
        pltpu.make_async_remote_copy(
            src_ref=send_buf.at[to],
            dst_ref=recv_buf.at[slot],
            send_sem=stack_send,
            recv_sem=stack_recv,
            device_id={"sta": to},
            device_id_type=MESH,
        ).start()
    own = send_buf[me_s].astype(jnp.float32)
    arrived = recv_buf.at[pl.ds(0, len(steps))]
    pltpu.make_async_copy(arrived, arrived, stack_recv).wait()
    out_ref[0] = own + jnp.sum(arrived[...].astype(jnp.float32), axis=0)
    pltpu.make_async_copy(arrived, arrived, stack_send).wait()


def shards(n_sta, n_tpl, waveform, fir_taps, templates, presence, moveout):
    stations, segment = waveform.shape
    n_rows, _, lags = templates.shape
    own_rows = n_rows // n_sta
    out_len = segment * n_tpl - lags - SHIFT_MOST
    lag_blocks = lags // BLK
    hbm = pl.BlockSpec(memory_space=pl.ANY)
    vmem = pl.BlockSpec(memory_space=pltpu.VMEM)
    return pl.pallas_call(
        functools.partial(kernel, n_sta, n_tpl),
        out_shape=pltpu.VMEM((1, own_rows, out_len), jnp.float32),
        in_specs=[hbm] * 5,
        out_specs=vmem,
        scratch_shapes=[
            pltpu.VMEM((n_tpl, stations, segment), jnp.float32),
            pltpu.VMEM((lag_blocks, n_rows, stations, BLK), jnp.bfloat16),
            pltpu.VMEM((2, n_rows * stations, BLK), jnp.float32),
            pltpu.VMEM((stations, lag_blocks // 2, n_rows, 2 * BLK), jnp.bfloat16),
            pltpu.VMEM((n_sta, own_rows, out_len), jnp.bfloat16),
            pltpu.VMEM((n_sta, own_rows, out_len), jnp.bfloat16),
            pltpu.SMEM((1, fir_taps.shape[0]), jnp.float32),
            pltpu.VMEM((stations, n_rows), jnp.int32),
            pltpu.VMEM((stations, n_rows), jnp.int32),
            pltpu.SemaphoreType.DMA((1 + lag_blocks,)),
            pltpu.SemaphoreType.DMA((3,)),
            pltpu.SemaphoreType.REGULAR((5,)),
            pltpu.SemaphoreType.DMA((n_tpl - 1,)),
            pltpu.SemaphoreType.DMA((n_tpl - 1,)),
            pltpu.SemaphoreType.DMA,
            pltpu.SemaphoreType.DMA,
        ],
        compiler_params=pltpu.CompilerParams(collective_id=0, has_side_effects=True),
    )(waveform, fir_taps[None, :], templates, presence.T, moveout.T)


def solution(mesh):
    placed = (P("sta", "tpl"), P(), P("tpl", "sta", None), P("tpl", "sta"), P("tpl", "sta"))
    return jax.shard_map(
        functools.partial(shards, mesh.shape["sta"], mesh.shape["tpl"]),
        mesh=mesh,
        in_specs=placed,
        out_specs=P("tpl", "sta", None),
        check_vma=False,
    )
```

```python
import functools

import jax
import jax.numpy as jnp
from jax import lax
from jax.experimental import pallas as pl
from jax.experimental.pallas import tpu as pltpu
from jax.sharding import PartitionSpec as P

BLK = 128
SHIFT_MOST = 128
EPSILON = 1e-06
MESH = pl.DeviceIdType.MESH


def lane_gather(values, index):
    return jnp.take_along_axis(values, index, axis=1, mode="promise_in_bounds")


def sta_dims(n_sta):
    return {64: (2, 8, 4), 8: (2, 2, 2), 4: (2, 2, 1)}.get(n_sta, (1, n_sta, 1))


def sta_offsets(dims):
    steps = [(dx, dz, dy) for dx in range(dims[0]) for dz in range(dims[1]) for dy in range(dims[2])][1:]
    far = {step: sum(min(d, n - d) for d, n in zip(step, dims)) for step in steps}
    return {step: far[step] for step in sorted(steps, key=lambda step: -far[step])}


def peer(me, step, dims):
    x, rest = me // (dims[1] * dims[2]), me % (dims[1] * dims[2])
    z, y = rest // dims[2], rest % dims[2]
    x = (x + step[0]) % dims[0]
    z = (z + step[1]) % dims[1]
    y = (y + step[2]) % dims[2]
    return (x * dims[1] + z) * dims[2] + y


def kernel(
    n_sta,
    n_tpl,
    wave_ref,
    fir_hbm,
    tpl_ref,
    pres_hbm,
    mov_hbm,
    out_ref,
    wave_buf,
    tpl_raw,
    rows32,
    tpl_split,
    send_buf,
    recv_buf,
    fir_ref,
    pres_ref,
    mov_ref,
    local_sem,
    small_sem,
    chain_sem,
    wave_send,
    wave_recv,
    stack_send,
    stack_recv,
):
    me_s, me_t = lax.axis_index("sta"), lax.axis_index("tpl")
    dims = sta_dims(n_sta)
    steps = sta_offsets(dims)
    stations = wave_ref.shape[0]
    n_rows = tpl_ref.shape[0]
    lag_blocks = tpl_ref.shape[2] // BLK
    own_rows = n_rows // n_sta
    seg_blocks = wave_ref.shape[1] // BLK
    wave_blocks = seg_blocks * n_tpl
    time_blocks = wave_blocks - lag_blocks
    out_blocks = time_blocks - 1

    def ring(distance):
        return [step for step, hops in steps.items() if hops == distance]

    near = ring(1)
    chain = [ring(1), ring(2), ring(3)]

    def tell(sem, steps):
        for step in steps:
            pl.semaphore_signal(sem, inc=1, device_id={"sta": peer(me_s, step, dims)}, device_id_type=MESH)

    def hear(stage):
        if chain[stage]:
            pl.semaphore_wait(chain_sem.at[stage], len(chain[stage]))
        if stage + 1 < len(chain):
            tell(chain_sem.at[stage + 1], chain[stage + 1])

    barrier = pltpu.get_barrier_semaphore()
    for step in range(n_tpl - 1, 0, -1):
        pl.semaphore_signal(barrier, inc=1, device_id={"tpl": lax.rem(me_t + step, n_tpl)}, device_id_type=MESH)
    tell(barrier, near)

    own_wave = pltpu.make_async_copy(wave_ref, wave_buf.at[me_t], local_sem.at[0])
    own_wave.start()
    small_copies = [
        pltpu.make_async_copy(mov_hbm, mov_ref, small_sem.at[0]),
        pltpu.make_async_copy(pres_hbm, pres_ref, small_sem.at[1]),
        pltpu.make_async_copy(fir_hbm, fir_ref, small_sem.at[2]),
    ]
    for copy in small_copies:
        copy.start()
    tpl_copies = []
    for b in range(lag_blocks):
        tpl_copies.append(
            pltpu.make_async_copy(
                tpl_ref.at[:, :, pl.ds(b * BLK, BLK)], tpl_raw.at[b], local_sem.at[1 + b]
            )
        )
        tpl_copies[-1].start()

    pl.semaphore_wait(barrier, n_tpl - 1 + len(near))
    own_wave.wait()
    wave_copies = []
    for step in range(1, n_tpl):
        wave_copies.append(
            pltpu.make_async_remote_copy(
                src_ref=wave_buf.at[me_t],
                dst_ref=wave_buf.at[me_t],
                send_sem=wave_send.at[step - 1],
                recv_sem=wave_recv.at[step - 1],
                device_id={"tpl": lax.rem(me_t + step, n_tpl)},
                device_id_type=MESH,
            )
        )
        wave_copies[-1].start()
    tell(chain_sem.at[0], chain[0])

    row_view = tpl_raw.reshape(lag_blocks, n_rows * stations, BLK)
    squares = [jnp.zeros((n_rows, BLK), jnp.float32) for _ in range(stations)]
    for b in range(lag_blocks):
        tpl_copies[b].wait()
        rows32[b % 2] = row_view[b].astype(jnp.float32)
        for s in range(stations):
            part = rows32[b % 2, pl.ds(s, n_rows, stride=stations), :]
            squares[s] = squares[s] + part * part
            tpl_split[s, lag_blocks // 2 - 1 - b // 2, :, (b % 2) * BLK : (b % 2 + 1) * BLK] = part.astype(
                jnp.bfloat16
            )

    hear(0)
    for copy in small_copies:
        copy.wait()
    lane = lax.broadcasted_iota(jnp.int32, (n_rows, BLK), 1)
    weights, gather_at, first_block = [], [], []
    for s in range(stations):
        norm = jnp.sqrt(jnp.sum(squares[s], axis=1, keepdims=True) + EPSILON)
        moved = jnp.transpose(jnp.broadcast_to(mov_ref[s : s + 1, :], (BLK, n_rows)))
        present = jnp.transpose(jnp.broadcast_to(pres_ref[s : s + 1, :].astype(jnp.float32), (BLK, n_rows)))
        weights.append(present / norm)
        position = lane + moved
        gather_at.append(position & (BLK - 1))
        first_block.append(position < BLK)

    hear(1)
    for copy in wave_copies:
        copy.wait()

    pieces = [
        wave_buf[c // seg_blocks, :, (c % seg_blocks) * BLK : (c % seg_blocks + 1) * BLK] for c in range(wave_blocks)
    ]
    now = jnp.concatenate(pieces, axis=0)
    before = jnp.concatenate([jnp.zeros((stations, BLK), jnp.float32)] + pieces[:-1], axis=0)
    row_lane = lax.broadcasted_iota(jnp.int32, now.shape, 1)
    sums = [now * fir_ref[0, 0], None]
    for i in range(1, fir_ref.shape[1]):
        term = pltpu.roll(jnp.where(row_lane < BLK - i, now, before), i, 1) * fir_ref[0, i]
        sums[i % 2] = term if sums[i % 2] is None else sums[i % 2] + term
    filtered = (sums[0] + sums[1]).astype(jnp.bfloat16).astype(jnp.float32)

    power = filtered * filtered
    high = power.astype(jnp.bfloat16)
    low = (power - high.astype(jnp.float32)).astype(jnp.bfloat16)
    taken = lax.broadcasted_iota(jnp.int32, (BLK, BLK), 0)
    at = lax.broadcasted_iota(jnp.int32, (BLK, BLK), 1)
    rest = jnp.where(taken >= at, 1.0, 0.0)
    masks = jnp.concatenate([rest, 1.0 - rest, jnp.ones((BLK, BLK), jnp.float32)], axis=1)
    sums = jnp.dot(
        jnp.concatenate([high, low], axis=0), masks.astype(jnp.bfloat16), preferred_element_type=jnp.float32
    )
    sums = sums[: power.shape[0]] + sums[power.shape[0] :]
    span = stations * time_blocks
    energy = sums[:span, :BLK] + sums[stations * lag_blocks :, BLK : 2 * BLK]
    for b in range(1, lag_blocks):
        energy = energy + sums[stations * b : stations * b + span, 2 * BLK :]
    inverse = 1.0 / jnp.sqrt(energy)

    tall = 16
    hankel_at = lax.broadcasted_iota(jnp.int32, (tall, BLK), 0) + lax.broadcasted_iota(jnp.int32, (tall, BLK), 1)
    hankel_index = hankel_at & (BLK - 1)
    hankel_first = hankel_at < BLK
    tall_lane = lax.broadcasted_iota(jnp.int32, (tall, BLK), 1)
    stack = [None] * out_blocks
    for s in range(stations):
        turned = [
            lane_gather(
                jnp.broadcast_to(filtered[stations * c + s : stations * c + s + 1, :], (tall, BLK)), hankel_index
            )
            for c in range(wave_blocks)
        ]
        heads = [
            jnp.where(hankel_first, turned[c], turned[min(c + 1, wave_blocks - 1)]).astype(jnp.bfloat16)
            for c in range(wave_blocks)
        ]
        blocks = [
            jnp.concatenate(
                [heads[c]]
                + [
                    pltpu.roll(jnp.where(tall_lane < q, heads[c + 1], heads[c]), BLK - q, 1)
                    for q in range(tall, BLK, tall)
                ],
                axis=0,
            )
            for c in range(wave_blocks - 1)
        ]
        pairs = lag_blocks // 2
        time_pairs = time_blocks // 2
        raw = [None] * time_pairs
        for c in range(pairs + time_pairs - 1):
            tile = jnp.concatenate(
                [
                    jnp.concatenate([blocks[2 * c], blocks[2 * c + 1]], axis=1),
                    jnp.concatenate([blocks[2 * c + 1], blocks[2 * c + 2]], axis=1),
                ],
                axis=0,
            )
            used = [p for p in range(time_pairs) if 0 <= c - p < pairs]
            first = pairs - 1 - (c - used[0])
            rows = tpl_split[s, first : first + len(used)].reshape(len(used) * n_rows, 2 * BLK)
            product = jnp.dot(rows, tile, preferred_element_type=jnp.float32)
            for i, p in enumerate(used):
                part = product[i * n_rows : (i + 1) * n_rows]
                raw[p] = part if raw[p] is None else raw[p] + part
        moved = []
        for b in range(time_blocks):
            scaled = raw[b // 2][:, (b % 2) * BLK : (b % 2 + 1) * BLK] * inverse[stations * b + s : stations * b + s + 1]
            moved.append(lane_gather(scaled, gather_at[s]))
        for b in range(out_blocks):
            term = weights[s] * jnp.where(first_block[s], moved[b], moved[b + 1])
            stack[b] = term if stack[b] is None else stack[b] + term
    send_buf[...] = jnp.concatenate(stack, axis=1).astype(jnp.bfloat16).reshape(send_buf.shape)

    hear(2)
    for slot, step in enumerate(steps):
        to = peer(me_s, step, dims)
        pltpu.make_async_remote_copy(
            src_ref=send_buf.at[to],
            dst_ref=recv_buf.at[slot],
            send_sem=stack_send,
            recv_sem=stack_recv,
            device_id={"sta": to},
            device_id_type=MESH,
        ).start()
    own = send_buf[me_s].astype(jnp.float32)
    arrived = recv_buf.at[pl.ds(0, len(steps))]
    pltpu.make_async_copy(arrived, arrived, stack_recv).wait()
    out_ref[0] = own + jnp.sum(arrived[...].astype(jnp.float32), axis=0)
    pltpu.make_async_copy(arrived, arrived, stack_send).wait()


def shards(n_sta, n_tpl, waveform, fir_taps, templates, presence, moveout):
    stations, segment = waveform.shape
    n_rows, _, lags = templates.shape
    own_rows = n_rows // n_sta
    out_len = segment * n_tpl - lags - SHIFT_MOST
    lag_blocks = lags // BLK
    hbm = pl.BlockSpec(memory_space=pl.ANY)
    vmem = pl.BlockSpec(memory_space=pltpu.VMEM)
    return pl.pallas_call(
        functools.partial(kernel, n_sta, n_tpl),
        out_shape=pltpu.VMEM((1, own_rows, out_len), jnp.float32),
        in_specs=[hbm] * 5,
        out_specs=vmem,
        scratch_shapes=[
            pltpu.VMEM((n_tpl, stations, segment), jnp.float32),
            pltpu.VMEM((lag_blocks, n_rows, stations, BLK), jnp.bfloat16),
            pltpu.VMEM((2, n_rows * stations, BLK), jnp.float32),
            pltpu.VMEM((stations, lag_blocks // 2, n_rows, 2 * BLK), jnp.bfloat16),
            pltpu.VMEM((n_sta, own_rows, out_len), jnp.bfloat16),
            pltpu.VMEM((n_sta, own_rows, out_len), jnp.bfloat16),
            pltpu.SMEM((1, fir_taps.shape[0]), jnp.float32),
            pltpu.VMEM((stations, n_rows), jnp.int32),
            pltpu.VMEM((stations, n_rows), jnp.int32),
            pltpu.SemaphoreType.DMA((1 + lag_blocks,)),
            pltpu.SemaphoreType.DMA((3,)),
            pltpu.SemaphoreType.REGULAR((3,)),
            pltpu.SemaphoreType.DMA((n_tpl - 1,)),
            pltpu.SemaphoreType.DMA((n_tpl - 1,)),
            pltpu.SemaphoreType.DMA,
            pltpu.SemaphoreType.DMA,
        ],
        compiler_params=pltpu.CompilerParams(collective_id=0, has_side_effects=True),
    )(waveform, fir_taps[None, :], templates, presence.T, moveout.T)


def solution(mesh):
    placed = (P("sta", "tpl"), P(), P("tpl", "sta", None), P("tpl", "sta"), P("tpl", "sta"))
    return jax.shard_map(
        functools.partial(shards, mesh.shape["sta"], mesh.shape["tpl"]),
        mesh=mesh,
        in_specs=placed,
        out_specs=P("tpl", "sta", None),
        check_vma=False,
    )
```

```python
import functools

import jax
import jax.numpy as jnp
from jax import lax
from jax.experimental import pallas as pl
from jax.experimental.pallas import tpu as pltpu
from jax.sharding import PartitionSpec as P

BLK = 128
SHIFT_MOST = 128
EPSILON = 1e-06
MESH = pl.DeviceIdType.MESH


def lane_gather(values, index):
    return jnp.take_along_axis(values, index, axis=1, mode="promise_in_bounds")


def sta_dims(n_sta):
    return {64: (2, 8, 4), 8: (2, 2, 2), 4: (2, 2, 1)}.get(n_sta, (1, n_sta, 1))


def places(me, dims):
    x, rest = me // (dims[1] * dims[2]), me % (dims[1] * dims[2])
    z, y = rest // dims[2], rest % dims[2]
    xs = [((x + d) % dims[0]) * (dims[1] * dims[2]) for d in range(dims[0])]
    ys = [(y + d) % dims[2] for d in range(dims[2])]
    return z, lambda dx, dy, at: xs[dx] + ys[dy] + at * dims[2]


def nearest(z, planes, n):
    return min(planes, key=lambda p: min((z - p) % n, (p - z) % n))


def kernel(
    n_sta,
    n_tpl,
    wave_ref,
    fir_hbm,
    tpl_ref,
    pres_hbm,
    mov_hbm,
    out_ref,
    wave_buf,
    tpl_raw,
    rows32,
    tpl_split,
    send_buf,
    recv_buf,
    fir_ref,
    pres_ref,
    mov_ref,
    local_sem,
    small_sem,
    chain_sem,
    wave_send,
    wave_recv,
    stack_send,
    stack_recv,
):
    me_s, me_t = lax.axis_index("sta"), lax.axis_index("tpl")
    dims = sta_dims(n_sta)
    me_z, place = places(me_s, dims)
    early = list(range(max(1, dims[1] // 4)))
    late = list(range(len(early), dims[1]))
    plane = [(dx, dy) for dx in range(dims[0]) for dy in range(dims[2])]
    plane.sort(key=lambda step: -sum(min(d, n - d) for d, n in zip(step, (dims[0], dims[2]))))
    is_early = me_z < len(early)
    stations = wave_ref.shape[0]
    n_rows = tpl_ref.shape[0]
    lag_blocks = tpl_ref.shape[2] // BLK
    own_rows = n_rows // n_sta
    seg_blocks = wave_ref.shape[1] // BLK
    wave_blocks = seg_blocks * n_tpl
    time_blocks = wave_blocks - lag_blocks
    out_blocks = time_blocks - 1

    def each(planes, do):
        for step in plane:
            for at in planes:
                to = place(*step, at)
                if step == (0, 0):
                    pl.when(me_z != at)(functools.partial(do, to))
                else:
                    do(to)

    def tell(sem, to):
        pl.semaphore_signal(sem, inc=1, device_id={"sta": to}, device_id_type=MESH)

    barrier = pltpu.get_barrier_semaphore()
    for step in range(n_tpl - 1, 0, -1):
        pl.semaphore_signal(barrier, inc=1, device_id={"tpl": lax.rem(me_t + step, n_tpl)}, device_id_type=MESH)

    @pl.when(is_early)
    def _():
        each(late + early, functools.partial(tell, barrier))

    own_wave = pltpu.make_async_copy(wave_ref, wave_buf.at[me_t], local_sem.at[0])
    own_wave.start()
    small_copies = [
        pltpu.make_async_copy(mov_hbm, mov_ref, small_sem.at[0]),
        pltpu.make_async_copy(pres_hbm, pres_ref, small_sem.at[1]),
        pltpu.make_async_copy(fir_hbm, fir_ref, small_sem.at[2]),
    ]
    for copy in small_copies:
        copy.start()
    tpl_copies = []
    for b in range(lag_blocks):
        tpl_copies.append(
            pltpu.make_async_copy(
                tpl_ref.at[:, :, pl.ds(b * BLK, BLK)], tpl_raw.at[b], local_sem.at[1 + b]
            )
        )
        tpl_copies[-1].start()

    n_early = len(plane) * len(early)
    pl.semaphore_wait(barrier, n_tpl - 1 + n_early - is_early.astype(jnp.int32))
    own_wave.wait()
    wave_copies = []
    for step in range(1, n_tpl):
        wave_copies.append(
            pltpu.make_async_remote_copy(
                src_ref=wave_buf.at[me_t],
                dst_ref=wave_buf.at[me_t],
                send_sem=wave_send.at[step - 1],
                recv_sem=wave_recv.at[step - 1],
                device_id={"tpl": lax.rem(me_t + step, n_tpl)},
                device_id_type=MESH,
            )
        )
        wave_copies[-1].start()
    @pl.when(jnp.logical_not(is_early))
    def _():
        each(early, functools.partial(tell, chain_sem.at[0]))


    row_view = tpl_raw.reshape(lag_blocks, n_rows * stations, BLK)
    squares = [jnp.zeros((n_rows, BLK), jnp.float32) for _ in range(stations)]
    for b in range(lag_blocks):
        tpl_copies[b].wait()
        rows32[b % 2] = row_view[b].astype(jnp.float32)
        for s in range(stations):
            part = rows32[b % 2, pl.ds(s, n_rows, stride=stations), :]
            squares[s] = squares[s] + part * part
            tpl_split[s, lag_blocks // 2 - 1 - b // 2, :, (b % 2) * BLK : (b % 2 + 1) * BLK] = part.astype(
                jnp.bfloat16
            )

    for copy in small_copies:
        copy.wait()
    lane = lax.broadcasted_iota(jnp.int32, (n_rows, BLK), 1)
    weights, gather_at, first_block = [], [], []
    for s in range(stations):
        norm = jnp.sqrt(jnp.sum(squares[s], axis=1, keepdims=True) + EPSILON)
        moved = jnp.transpose(jnp.broadcast_to(mov_ref[s : s + 1, :], (BLK, n_rows)))
        present = jnp.transpose(jnp.broadcast_to(pres_ref[s : s + 1, :].astype(jnp.float32), (BLK, n_rows)))
        weights.append(present / norm)
        position = lane + moved
        gather_at.append(position & (BLK - 1))
        first_block.append(position < BLK)

    for copy in wave_copies:
        copy.wait_recv()

    pieces = [
        wave_buf[c // seg_blocks, :, (c % seg_blocks) * BLK : (c % seg_blocks + 1) * BLK] for c in range(wave_blocks)
    ]
    now = jnp.concatenate(pieces, axis=0)
    before = jnp.concatenate([jnp.zeros((stations, BLK), jnp.float32)] + pieces[:-1], axis=0)
    row_lane = lax.broadcasted_iota(jnp.int32, now.shape, 1)
    sums = [now * fir_ref[0, 0], None]
    for i in range(1, fir_ref.shape[1]):
        term = pltpu.roll(jnp.where(row_lane < BLK - i, now, before), i, 1) * fir_ref[0, i]
        sums[i % 2] = term if sums[i % 2] is None else sums[i % 2] + term
    filtered = (sums[0] + sums[1]).astype(jnp.bfloat16).astype(jnp.float32)

    power = filtered * filtered
    high = power.astype(jnp.bfloat16)
    low = (power - high.astype(jnp.float32)).astype(jnp.bfloat16)
    taken = lax.broadcasted_iota(jnp.int32, (BLK, BLK), 0)
    at = lax.broadcasted_iota(jnp.int32, (BLK, BLK), 1)
    rest = jnp.where(taken >= at, 1.0, 0.0)
    masks = jnp.concatenate([rest, 1.0 - rest, jnp.ones((BLK, BLK), jnp.float32)], axis=1)
    sums = jnp.dot(
        jnp.concatenate([high, low], axis=0), masks.astype(jnp.bfloat16), preferred_element_type=jnp.float32
    )
    sums = sums[: power.shape[0]] + sums[power.shape[0] :]
    span = stations * time_blocks
    energy = sums[:span, :BLK] + sums[stations * lag_blocks :, BLK : 2 * BLK]
    for b in range(1, lag_blocks):
        energy = energy + sums[stations * b : stations * b + span, 2 * BLK :]
    inverse = 1.0 / jnp.sqrt(energy)

    tall = 16
    hankel_at = lax.broadcasted_iota(jnp.int32, (tall, BLK), 0) + lax.broadcasted_iota(jnp.int32, (tall, BLK), 1)
    hankel_index = hankel_at & (BLK - 1)
    hankel_first = hankel_at < BLK
    tall_lane = lax.broadcasted_iota(jnp.int32, (tall, BLK), 1)
    stack = [None] * out_blocks
    for s in range(stations):
        turned = [
            lane_gather(
                jnp.broadcast_to(filtered[stations * c + s : stations * c + s + 1, :], (tall, BLK)), hankel_index
            )
            for c in range(wave_blocks)
        ]
        heads = [
            jnp.where(hankel_first, turned[c], turned[min(c + 1, wave_blocks - 1)]).astype(jnp.bfloat16)
            for c in range(wave_blocks)
        ]
        blocks = [
            jnp.concatenate(
                [heads[c]]
                + [
                    pltpu.roll(jnp.where(tall_lane < q, heads[c + 1], heads[c]), BLK - q, 1)
                    for q in range(tall, BLK, tall)
                ],
                axis=0,
            )
            for c in range(wave_blocks - 1)
        ]
        pairs = lag_blocks // 2
        time_pairs = time_blocks // 2
        raw = [None] * time_pairs
        for c in range(pairs + time_pairs - 1):
            tile = jnp.concatenate(
                [
                    jnp.concatenate([blocks[2 * c], blocks[2 * c + 1]], axis=1),
                    jnp.concatenate([blocks[2 * c + 1], blocks[2 * c + 2]], axis=1),
                ],
                axis=0,
            )
            used = [p for p in range(time_pairs) if 0 <= c - p < pairs]
            first = pairs - 1 - (c - used[0])
            rows = tpl_split[s, first : first + len(used)].reshape(len(used) * n_rows, 2 * BLK)
            product = jnp.dot(rows, tile, preferred_element_type=jnp.float32)
            for i, p in enumerate(used):
                part = product[i * n_rows : (i + 1) * n_rows]
                raw[p] = part if raw[p] is None else raw[p] + part
        moved = []
        for b in range(time_blocks):
            scaled = raw[b // 2][:, (b % 2) * BLK : (b % 2 + 1) * BLK] * inverse[stations * b + s : stations * b + s + 1]
            moved.append(lane_gather(scaled, gather_at[s]))
        for b in range(out_blocks):
            term = weights[s] * jnp.where(first_block[s], moved[b], moved[b + 1])
            stack[b] = term if stack[b] is None else stack[b] + term
    send_buf[...] = jnp.concatenate(stack, axis=1).astype(jnp.bfloat16).reshape(send_buf.shape)

    def send(to):
        pltpu.make_async_remote_copy(
            src_ref=send_buf.at[to],
            dst_ref=recv_buf.at[me_s],
            send_sem=stack_send,
            recv_sem=stack_recv,
            device_id={"sta": to},
            device_id_type=MESH,
        ).start()

    each(early, send)
    recv_buf[me_s] = send_buf[me_s]

    @pl.when(is_early)
    def _():
        pl.semaphore_wait(chain_sem.at[0], len(plane) * len(late))
        for at in late:
            @pl.when(me_z == nearest(at, early, dims[1]))
            def _():
                tell(chain_sem.at[1], place(0, 0, at))

    @pl.when(jnp.logical_not(is_early))
    def _():
        pl.semaphore_wait(chain_sem.at[1], 1)

    each(late, send)
    arrived = recv_buf.at[pl.ds(0, n_sta - 1)]
    pltpu.make_async_copy(arrived, arrived, stack_recv).wait()
    out_ref[0] = jnp.sum(recv_buf[...].astype(jnp.float32), axis=0)
    for copy in wave_copies:
        copy.wait_send()
    pltpu.make_async_copy(arrived, arrived, stack_send).wait()


def shards(n_sta, n_tpl, waveform, fir_taps, templates, presence, moveout):
    stations, segment = waveform.shape
    n_rows, _, lags = templates.shape
    own_rows = n_rows // n_sta
    out_len = segment * n_tpl - lags - SHIFT_MOST
    lag_blocks = lags // BLK
    hbm = pl.BlockSpec(memory_space=pl.ANY)
    vmem = pl.BlockSpec(memory_space=pltpu.VMEM)
    return pl.pallas_call(
        functools.partial(kernel, n_sta, n_tpl),
        out_shape=pltpu.VMEM((1, own_rows, out_len), jnp.float32),
        in_specs=[hbm] * 5,
        out_specs=vmem,
        scratch_shapes=[
            pltpu.VMEM((n_tpl, stations, segment), jnp.float32),
            pltpu.VMEM((lag_blocks, n_rows, stations, BLK), jnp.bfloat16),
            pltpu.VMEM((2, n_rows * stations, BLK), jnp.float32),
            pltpu.VMEM((stations, lag_blocks // 2, n_rows, 2 * BLK), jnp.bfloat16),
            pltpu.VMEM((n_sta, own_rows, out_len), jnp.bfloat16),
            pltpu.VMEM((n_sta, own_rows, out_len), jnp.bfloat16),
            pltpu.SMEM((1, fir_taps.shape[0]), jnp.float32),
            pltpu.VMEM((stations, n_rows), jnp.int32),
            pltpu.VMEM((stations, n_rows), jnp.int32),
            pltpu.SemaphoreType.DMA((1 + lag_blocks,)),
            pltpu.SemaphoreType.DMA((3,)),
            pltpu.SemaphoreType.REGULAR((2,)),
            pltpu.SemaphoreType.DMA((n_tpl - 1,)),
            pltpu.SemaphoreType.DMA((n_tpl - 1,)),
            pltpu.SemaphoreType.DMA,
            pltpu.SemaphoreType.DMA,
        ],
        compiler_params=pltpu.CompilerParams(collective_id=0, has_side_effects=True),
    )(waveform, fir_taps[None, :], templates, presence.T, moveout.T)


def solution(mesh):
    placed = (P("sta", "tpl"), P(), P("tpl", "sta", None), P("tpl", "sta"), P("tpl", "sta"))
    return jax.shard_map(
        functools.partial(shards, mesh.shape["sta"], mesh.shape["tpl"]),
        mesh=mesh,
        in_specs=placed,
        out_specs=P("tpl", "sta", None),
        check_vma=False,
    )
```

```python
import functools

import jax
import jax.numpy as jnp
from jax import lax
from jax.experimental import pallas as pl
from jax.experimental.pallas import tpu as pltpu
from jax.sharding import PartitionSpec as P

BLK = 128
SHIFT_MOST = 128
ROWS = 8
EPSILON = 1e-06
MESH = pl.DeviceIdType.MESH


def lane_gather(values, index):
    return lax.gather(
        values,
        index[..., None],
        lax.GatherDimensionNumbers(
            offset_dims=(),
            collapsed_slice_dims=(1,),
            start_index_map=(1,),
            operand_batching_dims=(0,),
            start_indices_batching_dims=(0,),
        ),
        slice_sizes=(1, 1),
        mode=lax.GatherScatterMode.PROMISE_IN_BOUNDS,
    )


def split3(values):
    high = values.astype(jnp.bfloat16)
    rest = values - high.astype(jnp.float32)
    middle = rest.astype(jnp.bfloat16)
    low = (rest - middle.astype(jnp.float32)).astype(jnp.bfloat16)
    return [high, middle, low]


def sta_dims(n_sta):
    return {64: (2, 8, 4), 8: (2, 2, 2), 4: (2, 2, 1)}.get(n_sta, (1, n_sta, 1))


def places(me, dims):
    x, rest = me // (dims[1] * dims[2]), me % (dims[1] * dims[2])
    z, y = rest // dims[2], rest % dims[2]
    xs = [((x + d) % dims[0]) * (dims[1] * dims[2]) for d in range(dims[0])]
    ys = [(y + d) % dims[2] for d in range(dims[2])]
    return z, lambda dx, dy, at: xs[dx] + ys[dy] + at * dims[2]


def nearest(z, planes, n):
    return min(planes, key=lambda p: min((z - p) % n, (p - z) % n))


def kernel(
    n_sta,
    n_tpl,
    wave_ref,
    fir_hbm,
    tpl_ref,
    pres_hbm,
    mov_hbm,
    recv_buf,
    wave_buf,
    tpl_raw,
    rows32,
    tpl_split,
    raw_buf,
    moved_ref,
    weight_ref,
    send_buf,
    taps_ref,
    fir_ref,
    pres_ref,
    mov_ref,
    local_sem,
    small_sem,
    chain_sem,
    wave_send,
    wave_recv,
    stack_send,
    stack_recv,
):
    me_s, me_t = lax.axis_index("sta"), lax.axis_index("tpl")
    dims = sta_dims(n_sta)
    me_z, place = places(me_s, dims)
    early = list(range(max(1, 3 * dims[1] // 8)))
    late = list(range(len(early), dims[1]))
    plane = [(dx, dy) for dx in range(dims[0]) for dy in range(dims[2])]
    plane.sort(key=lambda step: -sum(min(d, n - d) for d, n in zip(step, (dims[0], dims[2]))))
    is_early = me_z < len(early)
    stations = wave_ref.shape[0]
    n_rows = tpl_ref.shape[0]
    lag_blocks = tpl_ref.shape[2] // BLK
    own_rows = n_rows // n_sta
    seg_blocks = wave_ref.shape[1] // BLK
    wave_blocks = seg_blocks * n_tpl
    time_blocks = wave_blocks - lag_blocks
    out_blocks = time_blocks - 1

    def each(planes, do):
        for step in plane:
            for at in planes:
                to = place(*step, at)
                if step == (0, 0):
                    pl.when(me_z != at)(functools.partial(do, to))
                else:
                    do(to)

    def tell(sem, to):
        pl.semaphore_signal(sem, inc=1, device_id={"sta": to}, device_id_type=MESH)

    barrier = pltpu.get_barrier_semaphore()
    for step in range(n_tpl - 1, 0, -1):
        pl.semaphore_signal(barrier, inc=1, device_id={"tpl": lax.rem(me_t + step, n_tpl)}, device_id_type=MESH)

    @pl.when(is_early)
    def _():
        each(late + early, functools.partial(tell, barrier))

    own_wave = pltpu.make_async_copy(wave_ref, wave_buf.at[me_t], local_sem.at[0])
    own_wave.start()
    small_copies = [
        pltpu.make_async_copy(mov_hbm, mov_ref, small_sem.at[0]),
        pltpu.make_async_copy(pres_hbm, pres_ref, small_sem.at[1]),
        pltpu.make_async_copy(fir_hbm, fir_ref, small_sem.at[2]),
    ]
    for copy in small_copies:
        copy.start()
    tpl_copies = []
    for b in range(lag_blocks):
        tpl_copies.append(
            pltpu.make_async_copy(
                tpl_ref.at[:, :, pl.ds(b * BLK, BLK)], tpl_raw.at[b], local_sem.at[1 + b]
            )
        )
        tpl_copies[-1].start()

    n_early = len(plane) * len(early)
    pl.semaphore_wait(barrier, n_tpl - 1 + n_early - is_early.astype(jnp.int32))
    own_wave.wait()
    wave_copies = []
    for step in range(1, n_tpl):
        wave_copies.append(
            pltpu.make_async_remote_copy(
                src_ref=wave_buf.at[me_t],
                dst_ref=wave_buf.at[me_t],
                send_sem=wave_send.at[step - 1],
                recv_sem=wave_recv.at[step - 1],
                device_id={"tpl": lax.rem(me_t + step, n_tpl)},
                device_id_type=MESH,
            )
        )
        wave_copies[-1].start()
    @pl.when(jnp.logical_not(is_early))
    def _():
        each(early, functools.partial(tell, chain_sem.at[0]))


    row_view = tpl_raw.reshape(lag_blocks, n_rows * stations, BLK)
    squares = [jnp.zeros((n_rows, BLK), jnp.float32) for _ in range(stations)]
    for b in range(lag_blocks):
        tpl_copies[b].wait()
        rows32[b % 2] = row_view[b].astype(jnp.float32)
        for s in range(stations):
            part = rows32[b % 2, pl.ds(s, n_rows, stride=stations), :]
            squares[s] = squares[s] + part * part
            tpl_split[s, lag_blocks // 2 - 1 - b // 2, :, (b % 2) * BLK : (b % 2 + 1) * BLK] = part.astype(
                jnp.bfloat16
            )

    for copy in small_copies:
        copy.wait()
    taps = jnp.concatenate([fir_ref[...], jnp.zeros((1, BLK - fir_ref.shape[1]), jnp.float32)], axis=1)
    from_at = lax.broadcasted_iota(jnp.int32, (BLK, BLK), 0)
    to_at = lax.broadcasted_iota(jnp.int32, (BLK, BLK), 1)
    turned = lane_gather(jnp.broadcast_to(taps, (BLK, BLK)), (to_at - from_at) & (BLK - 1))
    matrix = jnp.concatenate(
        [jnp.where(to_at >= from_at, turned, 0.0), jnp.where(to_at >= from_at, 0.0, turned)], axis=0
    )
    taps_ref[...] = jnp.concatenate(split3(matrix), axis=1)
    for s in range(stations):
        norm = jnp.sqrt(jnp.sum(squares[s], axis=1, keepdims=True) + EPSILON)
        moved = jnp.transpose(jnp.broadcast_to(mov_ref[s : s + 1, :], (BLK, n_rows)))
        present = jnp.transpose(jnp.broadcast_to(pres_ref[s : s + 1, :].astype(jnp.float32), (BLK, n_rows)))
        weight_ref[s] = present / norm
        moved_ref[s] = moved

    for copy in wave_copies:
        copy.wait_recv()

    pieces = [
        wave_buf[c // seg_blocks, :, (c % seg_blocks) * BLK : (c % seg_blocks + 1) * BLK] for c in range(wave_blocks)
    ]
    now = jnp.concatenate(pieces, axis=0)
    before = jnp.concatenate([jnp.zeros((stations, BLK), jnp.float32)] + pieces[:-1], axis=0)
    parts = split3(jnp.concatenate([now, before], axis=1))
    n = now.shape[0]
    products = jnp.dot(jnp.concatenate(parts, axis=0), taps_ref[...], preferred_element_type=jnp.float32)
    filtered = jnp.zeros((n, BLK), jnp.float32)
    for total in (2, 1, 0):
        for i in range(total + 1):
            filtered = filtered + products[i * n : (i + 1) * n, (total - i) * BLK : (total - i + 1) * BLK]
    filtered = filtered.astype(jnp.bfloat16).astype(jnp.float32)

    power = filtered * filtered
    high = power.astype(jnp.bfloat16)
    low = (power - high.astype(jnp.float32)).astype(jnp.bfloat16)
    taken = lax.broadcasted_iota(jnp.int32, (BLK, BLK), 0)
    at = lax.broadcasted_iota(jnp.int32, (BLK, BLK), 1)
    rest = jnp.where(taken >= at, 1.0, 0.0)
    masks = jnp.concatenate([rest, 1.0 - rest, jnp.ones((BLK, BLK), jnp.float32)], axis=1)
    sums = jnp.dot(
        jnp.concatenate([high, low], axis=0), masks.astype(jnp.bfloat16), preferred_element_type=jnp.float32
    )
    sums = sums[: power.shape[0]] + sums[power.shape[0] :]
    span = stations * time_blocks
    energy = sums[:span, :BLK] + sums[stations * lag_blocks :, BLK : 2 * BLK]
    for b in range(1, lag_blocks):
        energy = energy + sums[stations * b : stations * b + span, 2 * BLK :]
    inverse = 1.0 / jnp.sqrt(energy)

    tall = 16
    hankel_at = lax.broadcasted_iota(jnp.int32, (tall, BLK), 0) + lax.broadcasted_iota(jnp.int32, (tall, BLK), 1)
    hankel_index = hankel_at & (BLK - 1)
    hankel_first = hankel_at < BLK
    tall_lane = lax.broadcasted_iota(jnp.int32, (tall, BLK), 1)
    for s in range(stations):
        turned = [
            lane_gather(
                jnp.broadcast_to(filtered[stations * c + s : stations * c + s + 1, :], (tall, BLK)), hankel_index
            )
            for c in range(wave_blocks)
        ]
        heads = [
            jnp.where(hankel_first, turned[c], turned[min(c + 1, wave_blocks - 1)]).astype(jnp.bfloat16)
            for c in range(wave_blocks)
        ]
        blocks = [
            jnp.concatenate(
                [heads[c]]
                + [
                    pltpu.roll(jnp.where(tall_lane < q, heads[c + 1], heads[c]), BLK - q, 1)
                    for q in range(tall, BLK, tall)
                ],
                axis=0,
            )
            for c in range(wave_blocks - 1)
        ]
        pairs = lag_blocks // 2
        time_pairs = time_blocks // 2
        raw = [None] * time_pairs
        for c in range(pairs + time_pairs - 1):
            tile = jnp.concatenate(
                [
                    jnp.concatenate([blocks[2 * c], blocks[2 * c + 1]], axis=1),
                    jnp.concatenate([blocks[2 * c + 1], blocks[2 * c + 2]], axis=1),
                ],
                axis=0,
            )
            used = [p for p in range(time_pairs) if 0 <= c - p < pairs]
            first = pairs - 1 - (c - used[0])
            rows = tpl_split[s, first : first + len(used)].reshape(len(used) * n_rows, 2 * BLK)
            product = jnp.dot(rows, tile, preferred_element_type=jnp.float32)
            for i, p in enumerate(used):
                part = product[i * n_rows : (i + 1) * n_rows]
                raw[p] = part if raw[p] is None else raw[p] + part
        for p in range(time_pairs):
            raw_buf[s, p] = raw[p]

    scales = [
        [jnp.broadcast_to(inverse[stations * b + s : stations * b + s + 1], (ROWS, BLK)) for b in range(time_blocks)]
        for s in range(stations)
    ]
    row_lane = lax.broadcasted_iota(jnp.int32, (ROWS, BLK), 1)
    def shift(top):
        halves = []
        for at in (top, top + ROWS):
            stack = [None] * out_blocks
            for s in range(stations):
                moved = moved_ref[s, at : at + ROWS]
                weight = weight_ref[s, at : at + ROWS]
                index = (row_lane + moved) & (BLK - 1)
                stay = row_lane >= moved
                scaled = [
                    raw_buf[s, b // 2, at : at + ROWS, (b % 2) * BLK : (b % 2 + 1) * BLK] * scales[s][b]
                    for b in range(time_blocks)
                ]
                for b in range(out_blocks):
                    term = weight * lane_gather(jnp.where(stay, scaled[b], scaled[b + 1]), index)
                    stack[b] = term if stack[b] is None else stack[b] + term
            halves.append(jnp.concatenate(stack, axis=1))
        rows = jnp.concatenate(halves, axis=0).astype(jnp.bfloat16)
        send_buf[top // own_rows : (top + 2 * ROWS) // own_rows] = rows.reshape(
            2 * ROWS // own_rows, own_rows, out_blocks * BLK
        )

    def has_early(top):
        owners = range(top // own_rows, (top + 2 * ROWS - 1) // own_rows + 1)
        return any(owner % (dims[1] * dims[2]) // dims[2] in early for owner in owners)

    tops = range(0, n_rows, 2 * ROWS)
    for top in tops:
        if has_early(top):
            shift(top)

    def send(to):
        pltpu.make_async_remote_copy(
            src_ref=send_buf.at[to],
            dst_ref=recv_buf.at[me_s],
            send_sem=stack_send,
            recv_sem=stack_recv,
            device_id={"sta": to},
            device_id_type=MESH,
        ).start()

    each(early, send)
    for top in tops:
        if not has_early(top):
            shift(top)
    recv_buf[me_s] = send_buf[me_s]

    @pl.when(is_early)
    def _():
        pl.semaphore_wait(chain_sem.at[0], len(plane) * len(late))
        for at in late:
            @pl.when(me_z == nearest(at, early, dims[1]))
            def _():
                tell(chain_sem.at[1], place(0, 0, at))

    @pl.when(jnp.logical_not(is_early))
    def _():
        pl.semaphore_wait(chain_sem.at[1], 1)

    each(late, send)
    arrived = recv_buf.at[pl.ds(0, n_sta - 1)]
    pltpu.make_async_copy(arrived, arrived, stack_recv).wait()
    for copy in wave_copies:
        copy.wait_send()
    pltpu.make_async_copy(arrived, arrived, stack_send).wait()


def add_kernel(parts_ref, out_ref):
    out_ref[0] = jnp.sum(parts_ref[...].astype(jnp.float32), axis=0)


def shards(n_sta, n_tpl, waveform, fir_taps, templates, presence, moveout):
    stations, segment = waveform.shape
    n_rows, _, lags = templates.shape
    own_rows = n_rows // n_sta
    out_len = segment * n_tpl - lags - SHIFT_MOST
    lag_blocks = lags // BLK
    time_pairs = (segment * n_tpl // BLK - lag_blocks) // 2
    hbm = pl.BlockSpec(memory_space=pl.ANY)
    vmem = pl.BlockSpec(memory_space=pltpu.VMEM)
    parts = pl.pallas_call(
        functools.partial(kernel, n_sta, n_tpl),
        out_shape=pltpu.VMEM((n_sta, own_rows, out_len), jnp.bfloat16),
        in_specs=[hbm] * 5,
        out_specs=vmem,
        scratch_shapes=[
            pltpu.VMEM((n_tpl, stations, segment), jnp.float32),
            pltpu.VMEM((lag_blocks, n_rows, stations, BLK), jnp.bfloat16),
            pltpu.VMEM((2, n_rows * stations, BLK), jnp.float32),
            pltpu.VMEM((stations, lag_blocks // 2, n_rows, 2 * BLK), jnp.bfloat16),
            pltpu.VMEM((stations, time_pairs, n_rows, 2 * BLK), jnp.float32),
            pltpu.VMEM((stations, n_rows, BLK), jnp.int32),
            pltpu.VMEM((stations, n_rows, BLK), jnp.float32),
            pltpu.VMEM((n_sta, own_rows, out_len), jnp.bfloat16),
            pltpu.VMEM((2 * BLK, 3 * BLK), jnp.bfloat16),
            pltpu.VMEM((1, fir_taps.shape[0]), jnp.float32),
            pltpu.VMEM((stations, n_rows), jnp.int32),
            pltpu.VMEM((stations, n_rows), jnp.int32),
            pltpu.SemaphoreType.DMA((1 + lag_blocks,)),
            pltpu.SemaphoreType.DMA((3,)),
            pltpu.SemaphoreType.REGULAR((2,)),
            pltpu.SemaphoreType.DMA((n_tpl - 1,)),
            pltpu.SemaphoreType.DMA((n_tpl - 1,)),
            pltpu.SemaphoreType.DMA,
            pltpu.SemaphoreType.DMA,
        ],
        compiler_params=pltpu.CompilerParams(
            collective_id=0, has_side_effects=True
        ),
    )(waveform, fir_taps[None, :], templates, presence.T, moveout.T)
    return pl.pallas_call(
        add_kernel,
        out_shape=jax.ShapeDtypeStruct((1, own_rows, out_len), jnp.float32),
        in_specs=[vmem],
        out_specs=vmem,
    )(pltpu.with_memory_space_constraint(parts, pltpu.VMEM))


def solution(mesh):
    placed = (P("sta", "tpl"), P(), P("tpl", "sta", None), P("tpl", "sta"), P("tpl", "sta"))
    return jax.shard_map(
        functools.partial(shards, mesh.shape["sta"], mesh.shape["tpl"]),
        mesh=mesh,
        in_specs=placed,
        out_specs=P("tpl", "sta", None),
        check_vma=False,
    )
```

```python
import functools

import jax
import jax.numpy as jnp
from jax import lax
from jax.experimental import pallas as pl
from jax.experimental.pallas import tpu as pltpu
from jax.sharding import PartitionSpec as P

BLK = 128
SHIFT_MOST = 128
ROWS = 8
EPSILON = 1e-06
MESH = pl.DeviceIdType.MESH


def lane_gather(values, index):
    return lax.gather(
        values,
        index[..., None],
        lax.GatherDimensionNumbers(
            offset_dims=(),
            collapsed_slice_dims=(1,),
            start_index_map=(1,),
            operand_batching_dims=(0,),
            start_indices_batching_dims=(0,),
        ),
        slice_sizes=(1, 1),
        mode=lax.GatherScatterMode.PROMISE_IN_BOUNDS,
    )


def split3(values):
    high = values.astype(jnp.bfloat16)
    rest = values - high.astype(jnp.float32)
    middle = rest.astype(jnp.bfloat16)
    low = (rest - middle.astype(jnp.float32)).astype(jnp.bfloat16)
    return [high, middle, low]


def sta_dims(n_sta):
    return {64: (2, 8, 4), 8: (2, 2, 2), 4: (2, 2, 1)}.get(n_sta, (1, n_sta, 1))


def places(me, dims):
    x, rest = me // (dims[1] * dims[2]), me % (dims[1] * dims[2])
    z, y = rest // dims[2], rest % dims[2]
    xs = [((x + d) % dims[0]) * (dims[1] * dims[2]) for d in range(dims[0])]
    ys = [(y + d) % dims[2] for d in range(dims[2])]
    return z, lambda dx, dy, at: xs[dx] + ys[dy] + at * dims[2]


def nearest(z, planes, n):
    return min(planes, key=lambda p: min((z - p) % n, (p - z) % n))


def kernel(
    n_sta,
    n_tpl,
    wave_ref,
    fir_hbm,
    tpl_ref,
    pres_hbm,
    mov_hbm,
    recv_buf,
    wave_buf,
    tpl_raw,
    rows32,
    tpl_split,
    raw_buf,
    filtered_buf,
    edge_buf,
    scale_buf,
    moved_ref,
    weight_ref,
    send_buf,
    taps_ref,
    fir_ref,
    pres_ref,
    mov_ref,
    local_sem,
    small_sem,
    chain_sem,
    wave_send,
    wave_recv,
    stack_send,
    stack_recv,
):
    me_s, me_t = lax.axis_index("sta"), lax.axis_index("tpl")
    dims = sta_dims(n_sta)
    me_z, place = places(me_s, dims)
    early = list(range(max(1, 3 * dims[1] // 8)))
    late = list(range(len(early), dims[1]))
    plane = [(dx, dy) for dx in range(dims[0]) for dy in range(dims[2])]
    plane.sort(key=lambda step: -sum(min(d, n - d) for d, n in zip(step, (dims[0], dims[2]))))
    is_early = me_z < len(early)
    stations = wave_ref.shape[0]
    n_rows = tpl_ref.shape[0]
    lag_blocks = tpl_ref.shape[2] // BLK
    own_rows = n_rows // n_sta
    seg_blocks = wave_ref.shape[1] // BLK
    wave_blocks = seg_blocks * n_tpl
    time_blocks = wave_blocks - lag_blocks
    out_blocks = time_blocks - 1

    def each(planes, do):
        for step in plane:
            for at in planes:
                to = place(*step, at)
                if step == (0, 0):
                    pl.when(me_z != at)(functools.partial(do, to))
                else:
                    do(to)

    def tell(sem, to):
        pl.semaphore_signal(sem, inc=1, device_id={"sta": to}, device_id_type=MESH)

    barrier = pltpu.get_barrier_semaphore()
    for step in range(n_tpl - 1, 0, -1):
        pl.semaphore_signal(barrier, inc=1, device_id={"tpl": lax.rem(me_t + step, n_tpl)}, device_id_type=MESH)

    @pl.when(is_early)
    def _():
        each(late + early, functools.partial(tell, barrier))

    own_wave = pltpu.make_async_copy(wave_ref, wave_buf.at[me_t], local_sem.at[0])
    own_wave.start()
    small_copies = [
        pltpu.make_async_copy(mov_hbm, mov_ref, small_sem.at[0]),
        pltpu.make_async_copy(pres_hbm, pres_ref, small_sem.at[1]),
        pltpu.make_async_copy(fir_hbm, fir_ref, small_sem.at[2]),
    ]
    for copy in small_copies:
        copy.start()
    tpl_copies = []
    for b in range(lag_blocks):
        tpl_copies.append(
            pltpu.make_async_copy(
                tpl_ref.at[:, :, pl.ds(b * BLK, BLK)], tpl_raw.at[b], local_sem.at[1 + b]
            )
        )
        tpl_copies[-1].start()

    n_early = len(plane) * len(early)
    pl.semaphore_wait(barrier, n_tpl - 1 + n_early - is_early.astype(jnp.int32))
    own_wave.wait()
    beside = me_t + 1 - 2 * lax.rem(me_t, 2)
    half = n_tpl // 2
    wave_peers = [beside, lax.rem(me_t + half, n_tpl), lax.rem(beside + half, n_tpl)]
    wave_copies = [
        pltpu.make_async_remote_copy(
            src_ref=wave_buf.at[me_t],
            dst_ref=wave_buf.at[me_t],
            send_sem=wave_send.at[k],
            recv_sem=wave_recv.at[k],
            device_id={"tpl": wave_peers[k]},
            device_id_type=MESH,
        )
        for k in (1, 2, 0)
    ]
    for copy in wave_copies:
        copy.start()
    @pl.when(jnp.logical_not(is_early))
    def _():
        each(early, functools.partial(tell, chain_sem.at[0]))


    row_view = tpl_raw.reshape(lag_blocks, n_rows * stations, BLK)
    squares = [jnp.zeros((n_rows, BLK), jnp.float32) for _ in range(stations)]
    for b in range(lag_blocks):
        tpl_copies[b].wait()
        rows32[b % 2] = row_view[b].astype(jnp.float32)
        for s in range(stations):
            part = rows32[b % 2, pl.ds(s, n_rows, stride=stations), :]
            squares[s] = squares[s] + part * part
            tpl_split[s, lag_blocks // 2 - 1 - b // 2, :, (b % 2) * BLK : (b % 2 + 1) * BLK] = part.astype(
                jnp.bfloat16
            )

    for copy in small_copies:
        copy.wait()
    taps = jnp.concatenate([fir_ref[...], jnp.zeros((1, BLK - fir_ref.shape[1]), jnp.float32)], axis=1)
    from_at = lax.broadcasted_iota(jnp.int32, (BLK, BLK), 0)
    to_at = lax.broadcasted_iota(jnp.int32, (BLK, BLK), 1)
    turned = lane_gather(jnp.broadcast_to(taps, (BLK, BLK)), (to_at - from_at) & (BLK - 1))
    matrix = jnp.concatenate(
        [jnp.where(to_at >= from_at, turned, 0.0), jnp.where(to_at >= from_at, 0.0, turned)], axis=0
    )
    taps_ref[...] = jnp.concatenate(split3(matrix), axis=1)
    for s in range(stations):
        norm = jnp.sqrt(jnp.sum(squares[s], axis=1, keepdims=True) + EPSILON)
        moved = jnp.transpose(jnp.broadcast_to(mov_ref[s : s + 1, :], (BLK, n_rows)))
        present = jnp.transpose(jnp.broadcast_to(pres_ref[s : s + 1, :].astype(jnp.float32), (BLK, n_rows)))
        weight_ref[s] = present / norm
        moved_ref[s] = moved

    def piece(c):
        return wave_buf[c // seg_blocks, :, (c % seg_blocks) * BLK : (c % seg_blocks + 1) * BLK]

    def filter_blocks(low, high):
        pieces = [piece(c) for c in range(low, high)]
        now = jnp.concatenate(pieces, axis=0)
        first = piece(low - 1) if low else jnp.zeros((stations, BLK), jnp.float32)
        before = jnp.concatenate([first] + pieces[:-1], axis=0)
        parts = split3(jnp.concatenate([now, before], axis=1))
        n = now.shape[0]
        products = jnp.dot(jnp.concatenate(parts, axis=0), taps_ref[...], preferred_element_type=jnp.float32)
        filtered = jnp.zeros((n, BLK), jnp.float32)
        for total in (2, 1, 0):
            for i in range(total + 1):
                filtered = filtered + products[i * n : (i + 1) * n, (total - i) * BLK : (total - i + 1) * BLK]
        return filtered.astype(jnp.bfloat16).astype(jnp.float32)

    def scales_of(filtered):
        power = filtered * filtered
        high = power.astype(jnp.bfloat16)
        low = (power - high.astype(jnp.float32)).astype(jnp.bfloat16)
        taken = lax.broadcasted_iota(jnp.int32, (BLK, BLK), 0)
        at = lax.broadcasted_iota(jnp.int32, (BLK, BLK), 1)
        rest = jnp.where(taken >= at, 1.0, 0.0)
        masks = jnp.concatenate([rest, 1.0 - rest, jnp.ones((BLK, BLK), jnp.float32)], axis=1)
        sums = jnp.dot(
            jnp.concatenate([high, low], axis=0), masks.astype(jnp.bfloat16), preferred_element_type=jnp.float32
        )
        sums = sums[: power.shape[0]] + sums[power.shape[0] :]
        span = stations * time_blocks
        energy = sums[:span, :BLK] + sums[stations * lag_blocks :, BLK : 2 * BLK]
        for b in range(1, lag_blocks):
            energy = energy + sums[stations * b : stations * b + span, 2 * BLK :]
        inverse = 1.0 / jnp.sqrt(energy)
        return [
            [jnp.broadcast_to(inverse[stations * b + s : stations * b + s + 1], (ROWS, BLK)) for b in range(time_blocks)]
            for s in range(stations)
        ]

    tall = 16
    pairs = lag_blocks // 2
    time_pairs = time_blocks // 2

    def hankel(filtered, low, high, s):
        at = lax.broadcasted_iota(jnp.int32, (tall, BLK), 0) + lax.broadcasted_iota(jnp.int32, (tall, BLK), 1)
        lane = lax.broadcasted_iota(jnp.int32, (tall, BLK), 1)
        turned = [
            lane_gather(
                jnp.broadcast_to(filtered[stations * c + s : stations * c + s + 1, :], (tall, BLK)), at & (BLK - 1)
            )
            for c in range(high + 1 - low)
        ]
        heads = [
            jnp.where(at < BLK, turned[c], turned[min(c + 1, high - low)]).astype(jnp.bfloat16)
            for c in range(high + 1 - low)
        ]
        return {
            low + c: jnp.concatenate(
                [heads[c]]
                + [
                    pltpu.roll(jnp.where(lane < q, heads[c + 1], heads[c]), BLK - q, 1)
                    for q in range(tall, BLK, tall)
                ],
                axis=0,
            )
            for c in range(high - low)
        }

    def products(blocks, low, high, s, raw):
        raw = list(raw)
        for c in range(low, high):
            tile = jnp.concatenate(
                [
                    jnp.concatenate([blocks[2 * c], blocks[2 * c + 1]], axis=1),
                    jnp.concatenate([blocks[2 * c + 1], blocks[2 * c + 2]], axis=1),
                ],
                axis=0,
            )
            used = [p for p in range(time_pairs) if 0 <= c - p < pairs]
            first = pairs - 1 - (c - used[0])
            rows = tpl_split[s, first : first + len(used)].reshape(len(used) * n_rows, 2 * BLK)
            product = jnp.dot(rows, tile, preferred_element_type=jnp.float32)
            for i, p in enumerate(used):
                part = product[i * n_rows : (i + 1) * n_rows]
                raw[p] = part if raw[p] is None else raw[p] + part
        for p in range(time_pairs):
            raw_buf[s, p] = raw[p]

    row_lane = lax.broadcasted_iota(jnp.int32, (ROWS, BLK), 1)

    def shift(top, scales):
        halves = []
        for at in (top, top + ROWS):
            stack = [None] * out_blocks
            for s in range(stations):
                moved = moved_ref[s, at : at + ROWS]
                weight = weight_ref[s, at : at + ROWS]
                index = (row_lane + moved) & (BLK - 1)
                stay = row_lane >= moved
                scaled = [
                    raw_buf[s, b // 2, at : at + ROWS, (b % 2) * BLK : (b % 2 + 1) * BLK] * scales[s][b]
                    for b in range(time_blocks)
                ]
                for b in range(out_blocks):
                    term = weight * lane_gather(jnp.where(stay, scaled[b], scaled[b + 1]), index)
                    stack[b] = term if stack[b] is None else stack[b] + term
            halves.append(jnp.concatenate(stack, axis=1))
        rows = jnp.concatenate(halves, axis=0).astype(jnp.bfloat16)
        send_buf[top // own_rows : (top + 2 * ROWS) // own_rows] = rows.reshape(
            2 * ROWS // own_rows, own_rows, out_blocks * BLK
        )

    def has_early(top):
        owners = range(top // own_rows, (top + 2 * ROWS - 1) // own_rows + 1)
        return any(owner % (dims[1] * dims[2]) // dims[2] in early for owner in owners)

    tops = range(0, n_rows, 2 * ROWS)

    def rest(low, before):
        start = 2 * low
        filtered = filter_blocks(0 if low == 0 else start + 2, wave_blocks)
        if low:
            filtered = jnp.concatenate([before, filtered], axis=0)
        scales = scales_of(filtered)
        for s in range(stations):
            if low:
                blocks = hankel(filtered[stations * (start + 1) :], start + 1, wave_blocks - 1, s)
                blocks[start] = edge_buf[s]
            else:
                blocks = hankel(filtered, 0, wave_blocks - 1, s)
            products(
                blocks,
                low,
                pairs + time_pairs - 1,
                s,
                [raw_buf[s, p] for p in range(time_pairs)] if low else [None] * time_pairs,
            )
        for s in range(stations):
            for b in range(time_blocks):
                scale_buf[s, b] = scales[s][b]
        for top in tops:
            if has_early(top):
                shift(top, scales)

    near_blocks = wave_blocks // 2
    near_pairs = (near_blocks - 2) // 2
    in_first = me_t < half
    wave_copies[2].wait_recv()

    @pl.when(in_first)
    def _():
        filtered = filter_blocks(0, near_blocks)
        filtered_buf[...] = filtered
        for s in range(stations):
            blocks = hankel(filtered, 0, near_blocks - 1, s)
            products(blocks, 0, near_pairs, s, [None] * time_pairs)
            edge_buf[s] = blocks[2 * near_pairs]

    for copy in wave_copies[:2]:
        copy.wait_recv()

    @pl.when(in_first)
    def _():
        rest(near_pairs, filtered_buf[...])

    @pl.when(jnp.logical_not(in_first))
    def _():
        rest(0, None)

    def send(to):
        pltpu.make_async_remote_copy(
            src_ref=send_buf.at[to],
            dst_ref=recv_buf.at[me_s],
            send_sem=stack_send,
            recv_sem=stack_recv,
            device_id={"sta": to},
            device_id_type=MESH,
        ).start()

    each(early, send)
    scales = [[scale_buf[s, b] for b in range(time_blocks)] for s in range(stations)]
    for top in tops:
        if not has_early(top):
            shift(top, scales)
    recv_buf[me_s] = send_buf[me_s]

    @pl.when(is_early)
    def _():
        pl.semaphore_wait(chain_sem.at[0], len(plane) * len(late))
        for at in late:
            @pl.when(me_z == nearest(at, early, dims[1]))
            def _():
                tell(chain_sem.at[1], place(0, 0, at))

    @pl.when(jnp.logical_not(is_early))
    def _():
        pl.semaphore_wait(chain_sem.at[1], 1)

    each(late, send)
    arrived = recv_buf.at[pl.ds(0, n_sta - 1)]
    pltpu.make_async_copy(arrived, arrived, stack_recv).wait()
    for copy in wave_copies:
        copy.wait_send()
    pltpu.make_async_copy(arrived, arrived, stack_send).wait()


def add_kernel(parts_ref, out_ref):
    out_ref[0] = jnp.sum(parts_ref[...].astype(jnp.float32), axis=0)


def shards(n_sta, n_tpl, waveform, fir_taps, templates, presence, moveout):
    stations, segment = waveform.shape
    n_rows, _, lags = templates.shape
    own_rows = n_rows // n_sta
    out_len = segment * n_tpl - lags - SHIFT_MOST
    lag_blocks = lags // BLK
    time_pairs = (segment * n_tpl // BLK - lag_blocks) // 2
    hbm = pl.BlockSpec(memory_space=pl.ANY)
    vmem = pl.BlockSpec(memory_space=pltpu.VMEM)
    parts = pl.pallas_call(
        functools.partial(kernel, n_sta, n_tpl),
        out_shape=pltpu.VMEM((n_sta, own_rows, out_len), jnp.bfloat16),
        in_specs=[hbm] * 5,
        out_specs=vmem,
        scratch_shapes=[
            pltpu.VMEM((n_tpl, stations, segment), jnp.float32),
            pltpu.VMEM((lag_blocks, n_rows, stations, BLK), jnp.bfloat16),
            pltpu.VMEM((2, n_rows * stations, BLK), jnp.float32),
            pltpu.VMEM((stations, lag_blocks // 2, n_rows, 2 * BLK), jnp.bfloat16),
            pltpu.VMEM((stations, time_pairs, n_rows, 2 * BLK), jnp.float32),
            pltpu.VMEM((stations * segment * n_tpl // (2 * BLK), BLK), jnp.float32),
            pltpu.VMEM((stations, BLK, BLK), jnp.bfloat16),
            pltpu.VMEM((stations, 2 * time_pairs, ROWS, BLK), jnp.float32),
            pltpu.VMEM((stations, n_rows, BLK), jnp.int32),
            pltpu.VMEM((stations, n_rows, BLK), jnp.float32),
            pltpu.VMEM((n_sta, own_rows, out_len), jnp.bfloat16),
            pltpu.VMEM((2 * BLK, 3 * BLK), jnp.bfloat16),
            pltpu.VMEM((1, fir_taps.shape[0]), jnp.float32),
            pltpu.VMEM((stations, n_rows), jnp.int32),
            pltpu.VMEM((stations, n_rows), jnp.int32),
            pltpu.SemaphoreType.DMA((1 + lag_blocks,)),
            pltpu.SemaphoreType.DMA((3,)),
            pltpu.SemaphoreType.REGULAR((2,)),
            pltpu.SemaphoreType.DMA((n_tpl - 1,)),
            pltpu.SemaphoreType.DMA((n_tpl - 1,)),
            pltpu.SemaphoreType.DMA,
            pltpu.SemaphoreType.DMA,
        ],
        compiler_params=pltpu.CompilerParams(
            collective_id=0, has_side_effects=True
        ),
    )(waveform, fir_taps[None, :], templates, presence.T, moveout.T)
    return pl.pallas_call(
        add_kernel,
        out_shape=jax.ShapeDtypeStruct((1, own_rows, out_len), jnp.float32),
        in_specs=[vmem],
        out_specs=vmem,
    )(pltpu.with_memory_space_constraint(parts, pltpu.VMEM))


def solution(mesh):
    placed = (P("sta", "tpl"), P(), P("tpl", "sta", None), P("tpl", "sta"), P("tpl", "sta"))
    return jax.shard_map(
        functools.partial(shards, mesh.shape["sta"], mesh.shape["tpl"]),
        mesh=mesh,
        in_specs=placed,
        out_specs=P("tpl", "sta", None),
        check_vma=False,
    )
```

```python
import functools

import jax
import jax.numpy as jnp
from jax import lax
from jax.experimental import pallas as pl
from jax.experimental.pallas import tpu as pltpu
from jax.sharding import PartitionSpec as P

BLK = 128
SHIFT_MOST = 128
ROWS = 8
EPSILON = 1e-06
MESH = pl.DeviceIdType.MESH


def lane_gather(values, index):
    return lax.gather(
        values,
        index[..., None],
        lax.GatherDimensionNumbers(
            offset_dims=(),
            collapsed_slice_dims=(1,),
            start_index_map=(1,),
            operand_batching_dims=(0,),
            start_indices_batching_dims=(0,),
        ),
        slice_sizes=(1, 1),
        mode=lax.GatherScatterMode.PROMISE_IN_BOUNDS,
    )


def split3(values):
    high = values.astype(jnp.bfloat16)
    rest = values - high.astype(jnp.float32)
    middle = rest.astype(jnp.bfloat16)
    low = (rest - middle.astype(jnp.float32)).astype(jnp.bfloat16)
    return [high, middle, low]


def sta_dims(n_sta):
    return {64: (2, 8, 4), 8: (2, 2, 2), 4: (2, 2, 1)}.get(n_sta, (1, n_sta, 1))


def places(me, dims):
    x, rest = me // (dims[1] * dims[2]), me % (dims[1] * dims[2])
    z, y = rest // dims[2], rest % dims[2]
    xs = [((x + d) % dims[0]) * (dims[1] * dims[2]) for d in range(dims[0])]
    ys = [(y + d) % dims[2] for d in range(dims[2])]
    return z, lambda dx, dy, at: xs[dx] + ys[dy] + at * dims[2]


def nearest(z, planes, n):
    return min(planes, key=lambda p: min((z - p) % n, (p - z) % n))


def kernel(
    n_sta,
    n_tpl,
    wave_ref,
    fir_hbm,
    tpl_ref,
    pres_hbm,
    mov_hbm,
    recv_buf,
    wave_buf,
    tpl_raw,
    rows32,
    tpl_split,
    raw_buf,
    filtered_buf,
    edge_buf,
    scale_buf,
    moved_ref,
    weight_ref,
    send_buf,
    taps_ref,
    fir_ref,
    pres_ref,
    mov_ref,
    local_sem,
    small_sem,
    chain_sem,
    wave_send,
    wave_recv,
    stack_send,
    stack_recv,
):
    me_s, me_t = lax.axis_index("sta"), lax.axis_index("tpl")
    dims = sta_dims(n_sta)
    me_z, place = places(me_s, dims)
    early = list(range(max(1, 3 * dims[1] // 8)))
    late = list(range(len(early), dims[1]))
    plane = [(dx, dy) for dx in range(dims[0]) for dy in range(dims[2])]
    plane.sort(key=lambda step: -sum(min(d, n - d) for d, n in zip(step, (dims[0], dims[2]))))
    is_early = me_z < len(early)
    stations = wave_ref.shape[0]
    n_rows = tpl_ref.shape[0]
    lag_blocks = tpl_ref.shape[2] // BLK
    own_rows = n_rows // n_sta
    seg_blocks = wave_ref.shape[1] // BLK
    wave_blocks = seg_blocks * n_tpl
    time_blocks = wave_blocks - lag_blocks
    out_blocks = time_blocks - 1

    def each(planes, do):
        for step in plane:
            for at in planes:
                to = place(*step, at)
                if step == (0, 0):
                    pl.when(me_z != at)(functools.partial(do, to))
                else:
                    do(to)

    def tell(sem, to):
        pl.semaphore_signal(sem, inc=1, device_id={"sta": to}, device_id_type=MESH)

    barrier = pltpu.get_barrier_semaphore()
    for step in range(n_tpl - 1, 0, -1):
        pl.semaphore_signal(barrier, inc=1, device_id={"tpl": lax.rem(me_t + step, n_tpl)}, device_id_type=MESH)

    @pl.when(is_early)
    def _():
        each(late + early, functools.partial(tell, barrier))

    own_wave = pltpu.make_async_copy(wave_ref, wave_buf.at[me_t], local_sem.at[0])
    own_wave.start()
    small_copies = [
        pltpu.make_async_copy(mov_hbm, mov_ref, small_sem.at[0]),
        pltpu.make_async_copy(pres_hbm, pres_ref, small_sem.at[1]),
        pltpu.make_async_copy(fir_hbm, fir_ref, small_sem.at[2]),
    ]
    for copy in small_copies:
        copy.start()
    tpl_copies = []
    for b in range(lag_blocks):
        tpl_copies.append(
            pltpu.make_async_copy(
                tpl_ref.at[:, :, pl.ds(b * BLK, BLK)], tpl_raw.at[b], local_sem.at[1 + b]
            )
        )
        tpl_copies[-1].start()

    n_early = len(plane) * len(early)
    pl.semaphore_wait(barrier, n_tpl - 1 + n_early - is_early.astype(jnp.int32))
    own_wave.wait()
    half = n_tpl // 2
    core = lax.rem(me_t, 2)
    across = lax.rem(me_t - core + half, n_tpl)
    wave_copies = [
        pltpu.make_async_remote_copy(
            src_ref=wave_buf.at[me_t],
            dst_ref=wave_buf.at[me_t],
            send_sem=wave_send.at[k],
            recv_sem=wave_recv.at[sem],
            device_id={"tpl": to},
            device_id_type=MESH,
        )
        for k, (to, sem) in enumerate(((across + 1, 1 + core), (across, 1 + core), (me_t + 1 - 2 * core, 0)))
    ]
    for copy in wave_copies:
        copy.start()

    def wave_wait(sem):
        pltpu.make_async_copy(wave_buf.at[0], wave_buf.at[0], wave_recv.at[sem]).wait()

    @pl.when(jnp.logical_not(is_early))
    def _():
        each(early, functools.partial(tell, chain_sem.at[0]))


    row_view = tpl_raw.reshape(lag_blocks, n_rows * stations, BLK)
    squares = [jnp.zeros((n_rows, BLK), jnp.float32) for _ in range(stations)]
    for b in range(lag_blocks):
        tpl_copies[b].wait()
        rows32[b % 2] = row_view[b].astype(jnp.float32)
        for s in range(stations):
            part = rows32[b % 2, pl.ds(s, n_rows, stride=stations), :]
            squares[s] = squares[s] + part * part
            tpl_split[s, lag_blocks // 2 - 1 - b // 2, :, (b % 2) * BLK : (b % 2 + 1) * BLK] = part.astype(
                jnp.bfloat16
            )

    for copy in small_copies:
        copy.wait()
    taps = jnp.concatenate([fir_ref[...], jnp.zeros((1, BLK - fir_ref.shape[1]), jnp.float32)], axis=1)
    from_at = lax.broadcasted_iota(jnp.int32, (BLK, BLK), 0)
    to_at = lax.broadcasted_iota(jnp.int32, (BLK, BLK), 1)
    turned = lane_gather(jnp.broadcast_to(taps, (BLK, BLK)), (to_at - from_at) & (BLK - 1))
    matrix = jnp.concatenate(
        [jnp.where(to_at >= from_at, turned, 0.0), jnp.where(to_at >= from_at, 0.0, turned)], axis=0
    )
    taps_ref[...] = jnp.concatenate(split3(matrix), axis=1)
    for s in range(stations):
        norm = jnp.sqrt(jnp.sum(squares[s], axis=1, keepdims=True) + EPSILON)
        moved = jnp.transpose(jnp.broadcast_to(mov_ref[s : s + 1, :], (BLK, n_rows)))
        present = jnp.transpose(jnp.broadcast_to(pres_ref[s : s + 1, :].astype(jnp.float32), (BLK, n_rows)))
        weight_ref[s] = present / norm
        moved_ref[s] = moved

    def piece(c):
        return wave_buf[c // seg_blocks, :, (c % seg_blocks) * BLK : (c % seg_blocks + 1) * BLK]

    def filter_blocks(low, high):
        pieces = [piece(c) for c in range(low, high)]
        now = jnp.concatenate(pieces, axis=0)
        first = piece(low - 1) if low else jnp.zeros((stations, BLK), jnp.float32)
        before = jnp.concatenate([first] + pieces[:-1], axis=0)
        parts = split3(jnp.concatenate([now, before], axis=1))
        n = now.shape[0]
        products = jnp.dot(jnp.concatenate(parts, axis=0), taps_ref[...], preferred_element_type=jnp.float32)
        filtered = jnp.zeros((n, BLK), jnp.float32)
        for total in (2, 1, 0):
            for i in range(total + 1):
                filtered = filtered + products[i * n : (i + 1) * n, (total - i) * BLK : (total - i + 1) * BLK]
        return filtered.astype(jnp.bfloat16).astype(jnp.float32)

    def scales_of(filtered):
        power = filtered * filtered
        high = power.astype(jnp.bfloat16)
        low = (power - high.astype(jnp.float32)).astype(jnp.bfloat16)
        taken = lax.broadcasted_iota(jnp.int32, (BLK, BLK), 0)
        at = lax.broadcasted_iota(jnp.int32, (BLK, BLK), 1)
        rest = jnp.where(taken >= at, 1.0, 0.0)
        masks = jnp.concatenate([rest, 1.0 - rest, jnp.ones((BLK, BLK), jnp.float32)], axis=1)
        sums = jnp.dot(
            jnp.concatenate([high, low], axis=0), masks.astype(jnp.bfloat16), preferred_element_type=jnp.float32
        )
        sums = sums[: power.shape[0]] + sums[power.shape[0] :]
        span = stations * time_blocks
        energy = sums[:span, :BLK] + sums[stations * lag_blocks :, BLK : 2 * BLK]
        for b in range(1, lag_blocks):
            energy = energy + sums[stations * b : stations * b + span, 2 * BLK :]
        inverse = 1.0 / jnp.sqrt(energy)
        return [
            [jnp.broadcast_to(inverse[stations * b + s : stations * b + s + 1], (ROWS, BLK)) for b in range(time_blocks)]
            for s in range(stations)
        ]

    tall = 16
    pairs = lag_blocks // 2
    time_pairs = time_blocks // 2

    def hankel(filtered, low, high, s):
        at = lax.broadcasted_iota(jnp.int32, (tall, BLK), 0) + lax.broadcasted_iota(jnp.int32, (tall, BLK), 1)
        lane = lax.broadcasted_iota(jnp.int32, (tall, BLK), 1)
        turned = [
            lane_gather(
                jnp.broadcast_to(filtered[stations * c + s : stations * c + s + 1, :], (tall, BLK)), at & (BLK - 1)
            )
            for c in range(high + 1 - low)
        ]
        heads = [
            jnp.where(at < BLK, turned[c], turned[min(c + 1, high - low)]).astype(jnp.bfloat16)
            for c in range(high + 1 - low)
        ]
        return {
            low + c: jnp.concatenate(
                [heads[c]]
                + [
                    pltpu.roll(jnp.where(lane < q, heads[c + 1], heads[c]), BLK - q, 1)
                    for q in range(tall, BLK, tall)
                ],
                axis=0,
            )
            for c in range(high - low)
        }

    def products(blocks, low, high, s, raw):
        raw = list(raw)
        for c in range(low, high):
            tile = jnp.concatenate(
                [
                    jnp.concatenate([blocks[2 * c], blocks[2 * c + 1]], axis=1),
                    jnp.concatenate([blocks[2 * c + 1], blocks[2 * c + 2]], axis=1),
                ],
                axis=0,
            )
            used = [p for p in range(time_pairs) if 0 <= c - p < pairs]
            first = pairs - 1 - (c - used[0])
            rows = tpl_split[s, first : first + len(used)].reshape(len(used) * n_rows, 2 * BLK)
            product = jnp.dot(rows, tile, preferred_element_type=jnp.float32)
            for i, p in enumerate(used):
                part = product[i * n_rows : (i + 1) * n_rows]
                raw[p] = part if raw[p] is None else raw[p] + part
        for p in range(time_pairs):
            raw_buf[s, p] = raw[p]

    row_lane = lax.broadcasted_iota(jnp.int32, (ROWS, BLK), 1)

    def shift(top, scales):
        halves = []
        for at in (top, top + ROWS):
            stack = [None] * out_blocks
            for s in range(stations):
                moved = moved_ref[s, at : at + ROWS]
                weight = weight_ref[s, at : at + ROWS]
                index = (row_lane + moved) & (BLK - 1)
                stay = row_lane >= moved
                scaled = [
                    raw_buf[s, b // 2, at : at + ROWS, (b % 2) * BLK : (b % 2 + 1) * BLK] * scales[s][b]
                    for b in range(time_blocks)
                ]
                for b in range(out_blocks):
                    term = weight * lane_gather(jnp.where(stay, scaled[b], scaled[b + 1]), index)
                    stack[b] = term if stack[b] is None else stack[b] + term
            halves.append(jnp.concatenate(stack, axis=1))
        rows = jnp.concatenate(halves, axis=0).astype(jnp.bfloat16)
        send_buf[top // own_rows : (top + 2 * ROWS) // own_rows] = rows.reshape(
            2 * ROWS // own_rows, own_rows, out_blocks * BLK
        )

    def of_planes(planes):
        return [
            top
            for top in range(0, n_rows, 2 * ROWS)
            if any(
                owner % (dims[1] * dims[2]) // dims[2] in planes
                for owner in range(top // own_rows, (top + 2 * ROWS - 1) // own_rows + 1)
            )
        ]

    waves = [early[:2], early[2:], late]
    tops = [of_planes(planes) for planes in waves]
    tops[1] = [top for top in tops[1] if top not in tops[0]]
    tops[2] = [top for top in tops[2] if top not in tops[0] + tops[1]]

    def rest(low, before):
        start = 2 * low
        filtered = filter_blocks(0 if low == 0 else start + 2, wave_blocks)
        if low:
            filtered = jnp.concatenate([before, filtered], axis=0)
        scales = scales_of(filtered)
        for s in range(stations):
            if low:
                blocks = hankel(filtered[stations * (start + 1) :], start + 1, wave_blocks - 1, s)
                blocks[start] = edge_buf[s]
            else:
                blocks = hankel(filtered, 0, wave_blocks - 1, s)
            products(
                blocks,
                low,
                pairs + time_pairs - 1,
                s,
                [raw_buf[s, p] for p in range(time_pairs)] if low else [None] * time_pairs,
            )
        for s in range(stations):
            for b in range(time_blocks):
                scale_buf[s, b] = scales[s][b]
        for top in tops[0]:
            shift(top, scales)

    near_blocks = wave_blocks // 2
    near_pairs = (near_blocks - 2) // 2
    in_first = me_t < half
    wave_wait(0)

    @pl.when(in_first)
    def _():
        filtered = filter_blocks(0, near_blocks)
        filtered_buf[...] = filtered
        for s in range(stations):
            blocks = hankel(filtered, 0, near_blocks - 1, s)
            products(blocks, 0, near_pairs, s, [None] * time_pairs)
            edge_buf[s] = blocks[2 * near_pairs]

    wave_wait(1)
    wave_wait(2)

    @pl.when(in_first)
    def _():
        rest(near_pairs, filtered_buf[...])

    @pl.when(jnp.logical_not(in_first))
    def _():
        rest(0, None)

    def send(to):
        pltpu.make_async_remote_copy(
            src_ref=send_buf.at[to],
            dst_ref=recv_buf.at[me_s],
            send_sem=stack_send,
            recv_sem=stack_recv,
            device_id={"sta": to},
            device_id_type=MESH,
        ).start()

    scales = [[scale_buf[s, b] for b in range(time_blocks)] for s in range(stations)]
    each(waves[0], send)
    for top in tops[1]:
        shift(top, scales)
    each(waves[1], send)
    for top in tops[2]:
        shift(top, scales)
    recv_buf[me_s] = send_buf[me_s]

    @pl.when(is_early)
    def _():
        pl.semaphore_wait(chain_sem.at[0], len(plane) * len(late))
        for at in late:
            @pl.when(me_z == nearest(at, early, dims[1]))
            def _():
                tell(chain_sem.at[1], place(0, 0, at))

    @pl.when(jnp.logical_not(is_early))
    def _():
        pl.semaphore_wait(chain_sem.at[1], 1)

    each(late, send)
    arrived = recv_buf.at[pl.ds(0, n_sta - 1)]
    pltpu.make_async_copy(arrived, arrived, stack_recv).wait()
    for copy in wave_copies:
        copy.wait_send()
    pltpu.make_async_copy(arrived, arrived, stack_send).wait()


def add_kernel(parts_ref, out_ref):
    out_ref[0] = jnp.sum(parts_ref[...].astype(jnp.float32), axis=0)


def shards(n_sta, n_tpl, waveform, fir_taps, templates, presence, moveout):
    stations, segment = waveform.shape
    n_rows, _, lags = templates.shape
    own_rows = n_rows // n_sta
    out_len = segment * n_tpl - lags - SHIFT_MOST
    lag_blocks = lags // BLK
    time_pairs = (segment * n_tpl // BLK - lag_blocks) // 2
    hbm = pl.BlockSpec(memory_space=pl.ANY)
    vmem = pl.BlockSpec(memory_space=pltpu.VMEM)
    parts = pl.pallas_call(
        functools.partial(kernel, n_sta, n_tpl),
        out_shape=pltpu.VMEM((n_sta, own_rows, out_len), jnp.bfloat16),
        in_specs=[hbm] * 5,
        out_specs=vmem,
        scratch_shapes=[
            pltpu.VMEM((n_tpl, stations, segment), jnp.float32),
            pltpu.VMEM((lag_blocks, n_rows, stations, BLK), jnp.bfloat16),
            pltpu.VMEM((2, n_rows * stations, BLK), jnp.float32),
            pltpu.VMEM((stations, lag_blocks // 2, n_rows, 2 * BLK), jnp.bfloat16),
            pltpu.VMEM((stations, time_pairs, n_rows, 2 * BLK), jnp.float32),
            pltpu.VMEM((stations * segment * n_tpl // (2 * BLK), BLK), jnp.float32),
            pltpu.VMEM((stations, BLK, BLK), jnp.bfloat16),
            pltpu.VMEM((stations, 2 * time_pairs, ROWS, BLK), jnp.float32),
            pltpu.VMEM((stations, n_rows, BLK), jnp.int32),
            pltpu.VMEM((stations, n_rows, BLK), jnp.float32),
            pltpu.VMEM((n_sta, own_rows, out_len), jnp.bfloat16),
            pltpu.VMEM((2 * BLK, 3 * BLK), jnp.bfloat16),
            pltpu.VMEM((1, fir_taps.shape[0]), jnp.float32),
            pltpu.VMEM((stations, n_rows), jnp.int32),
            pltpu.VMEM((stations, n_rows), jnp.int32),
            pltpu.SemaphoreType.DMA((1 + lag_blocks,)),
            pltpu.SemaphoreType.DMA((3,)),
            pltpu.SemaphoreType.REGULAR((2,)),
            pltpu.SemaphoreType.DMA((n_tpl - 1,)),
            pltpu.SemaphoreType.DMA((n_tpl - 1,)),
            pltpu.SemaphoreType.DMA,
            pltpu.SemaphoreType.DMA,
        ],
        compiler_params=pltpu.CompilerParams(
            collective_id=0, has_side_effects=True
        ),
    )(waveform, fir_taps[None, :], templates, presence.T, moveout.T)
    return pl.pallas_call(
        add_kernel,
        out_shape=jax.ShapeDtypeStruct((1, own_rows, out_len), jnp.float32),
        in_specs=[vmem],
        out_specs=vmem,
    )(pltpu.with_memory_space_constraint(parts, pltpu.VMEM))


def solution(mesh):
    placed = (P("sta", "tpl"), P(), P("tpl", "sta", None), P("tpl", "sta"), P("tpl", "sta"))
    return jax.shard_map(
        functools.partial(shards, mesh.shape["sta"], mesh.shape["tpl"]),
        mesh=mesh,
        in_specs=placed,
        out_specs=P("tpl", "sta", None),
        check_vma=False,
    )
```

```python
import functools

import jax
import jax.numpy as jnp
from jax import lax
from jax.experimental import pallas as pl
from jax.experimental.pallas import tpu as pltpu
from jax.sharding import PartitionSpec as P

BLK = 128
SHIFT_MOST = 128
ROWS = 8
EPSILON = 1e-06
MESH = pl.DeviceIdType.MESH


def lane_gather(values, index):
    return lax.gather(
        values,
        index[..., None],
        lax.GatherDimensionNumbers(
            offset_dims=(),
            collapsed_slice_dims=(1,),
            start_index_map=(1,),
            operand_batching_dims=(0,),
            start_indices_batching_dims=(0,),
        ),
        slice_sizes=(1, 1),
        mode=lax.GatherScatterMode.PROMISE_IN_BOUNDS,
    )


def split3(values):
    high = values.astype(jnp.bfloat16)
    rest = values - high.astype(jnp.float32)
    middle = rest.astype(jnp.bfloat16)
    low = (rest - middle.astype(jnp.float32)).astype(jnp.bfloat16)
    return [high, middle, low]


def sta_dims(n_sta):
    return {64: (2, 8, 4), 8: (2, 2, 2), 4: (2, 2, 1)}.get(n_sta, (1, n_sta, 1))


def places(me, dims):
    x, rest = me // (dims[1] * dims[2]), me % (dims[1] * dims[2])
    z, y = rest // dims[2], rest % dims[2]
    xs = [((x + d) % dims[0]) * (dims[1] * dims[2]) for d in range(dims[0])]
    ys = [(y + d) % dims[2] for d in range(dims[2])]
    return z, lambda dx, dy, at: xs[dx] + ys[dy] + at * dims[2]


def nearest(z, planes, n):
    return min(planes, key=lambda p: min((z - p) % n, (p - z) % n))


def kernel(
    n_sta,
    n_tpl,
    wave_ref,
    fir_hbm,
    tpl_ref,
    pres_hbm,
    mov_hbm,
    recv_buf,
    wave_buf,
    tpl_raw,
    rows32,
    tpl_split,
    raw_buf,
    filtered_buf,
    edge_buf,
    scale_buf,
    moved_ref,
    weight_ref,
    send_buf,
    taps_ref,
    fir_ref,
    pres_ref,
    mov_ref,
    local_sem,
    small_sem,
    chain_sem,
    wave_send,
    wave_recv,
    stack_send,
    stack_recv,
):
    me_s, me_t = lax.axis_index("sta"), lax.axis_index("tpl")
    dims = sta_dims(n_sta)
    me_z, place = places(me_s, dims)
    early = list(range(max(1, 3 * dims[1] // 8)))
    late = list(range(len(early), dims[1]))
    plane = [(dx, dy) for dx in range(dims[0]) for dy in range(dims[2])]
    plane.sort(key=lambda step: -sum(min(d, n - d) for d, n in zip(step, (dims[0], dims[2]))))
    is_early = me_z < len(early)
    stations = wave_ref.shape[0]
    n_rows = tpl_ref.shape[0]
    lag_blocks = tpl_ref.shape[2] // BLK
    own_rows = n_rows // n_sta
    seg_blocks = wave_ref.shape[1] // BLK
    wave_blocks = seg_blocks * n_tpl
    time_blocks = wave_blocks - lag_blocks
    out_blocks = time_blocks - 1

    def each(planes, do):
        for step in plane:
            for at in planes:
                to = place(*step, at)
                if step == (0, 0):
                    pl.when(me_z != at)(functools.partial(do, to))
                else:
                    do(to)

    def tell(sem, to):
        pl.semaphore_signal(sem, inc=1, device_id={"sta": to}, device_id_type=MESH)

    barrier = pltpu.get_barrier_semaphore()
    for step in range(n_tpl - 1, 0, -1):
        pl.semaphore_signal(barrier, inc=1, device_id={"tpl": lax.rem(me_t + step, n_tpl)}, device_id_type=MESH)

    @pl.when(is_early)
    def _():
        each(late + early, functools.partial(tell, barrier))

    own_wave = pltpu.make_async_copy(wave_ref, wave_buf.at[me_t], local_sem.at[0])
    own_wave.start()
    small_copies = [
        pltpu.make_async_copy(mov_hbm, mov_ref, small_sem.at[0]),
        pltpu.make_async_copy(pres_hbm, pres_ref, small_sem.at[1]),
        pltpu.make_async_copy(fir_hbm, fir_ref, small_sem.at[2]),
    ]
    for copy in small_copies:
        copy.start()
    tpl_copies = []
    for b in range(lag_blocks):
        tpl_copies.append(
            pltpu.make_async_copy(
                tpl_ref.at[:, :, pl.ds(b * BLK, BLK)], tpl_raw.at[b], local_sem.at[1 + b]
            )
        )
        tpl_copies[-1].start()

    n_early = len(plane) * len(early)
    pl.semaphore_wait(barrier, n_tpl - 1 + n_early - is_early.astype(jnp.int32))
    own_wave.wait()
    half = n_tpl // 2
    core = lax.rem(me_t, 2)
    across = lax.rem(me_t - core + half, n_tpl)
    wave_copies = [
        pltpu.make_async_remote_copy(
            src_ref=wave_buf.at[me_t],
            dst_ref=wave_buf.at[me_t],
            send_sem=wave_send.at[k],
            recv_sem=wave_recv.at[sem],
            device_id={"tpl": to},
            device_id_type=MESH,
        )
        for k, (to, sem) in enumerate(((across + 1, 1 + core), (across, 1 + core), (me_t + 1 - 2 * core, 0)))
    ]
    for copy in wave_copies:
        copy.start()

    def wave_wait(sem):
        pltpu.make_async_copy(wave_buf.at[0], wave_buf.at[0], wave_recv.at[sem]).wait()

    @pl.when(jnp.logical_not(is_early))
    def _():
        each(early, functools.partial(tell, chain_sem.at[0]))


    row_view = tpl_raw.reshape(lag_blocks, n_rows * stations, BLK)
    squares = [jnp.zeros((n_rows, BLK), jnp.float32) for _ in range(stations)]
    for b in range(lag_blocks):
        tpl_copies[b].wait()
        rows32[b % 2] = row_view[b].astype(jnp.float32)
        for s in range(stations):
            part = rows32[b % 2, pl.ds(s, n_rows, stride=stations), :]
            squares[s] = squares[s] + part * part
            tpl_split[s, lag_blocks // 2 - 1 - b // 2, :, (b % 2) * BLK : (b % 2 + 1) * BLK] = part.astype(
                jnp.bfloat16
            )

    for copy in small_copies:
        copy.wait()
    taps = jnp.concatenate([fir_ref[...], jnp.zeros((1, BLK - fir_ref.shape[1]), jnp.float32)], axis=1)
    from_at = lax.broadcasted_iota(jnp.int32, (BLK, BLK), 0)
    to_at = lax.broadcasted_iota(jnp.int32, (BLK, BLK), 1)
    turned = lane_gather(jnp.broadcast_to(taps, (BLK, BLK)), (to_at - from_at) & (BLK - 1))
    matrix = jnp.concatenate(
        [jnp.where(to_at >= from_at, turned, 0.0), jnp.where(to_at >= from_at, 0.0, turned)], axis=0
    )
    taps_ref[...] = jnp.concatenate(split3(matrix), axis=1)
    for s in range(stations):
        norm = jnp.sqrt(jnp.sum(squares[s], axis=1, keepdims=True) + EPSILON)
        moved = jnp.transpose(jnp.broadcast_to(mov_ref[s : s + 1, :], (BLK, n_rows)))
        present = jnp.transpose(jnp.broadcast_to(pres_ref[s : s + 1, :].astype(jnp.float32), (BLK, n_rows)))
        weight_ref[s] = present / norm
        moved_ref[s] = moved

    def piece(c):
        return wave_buf[c // seg_blocks, :, (c % seg_blocks) * BLK : (c % seg_blocks + 1) * BLK]

    def filter_blocks(low, high):
        pieces = [piece(c) for c in range(low, high)]
        now = jnp.concatenate(pieces, axis=0)
        first = piece(low - 1) if low else jnp.zeros((stations, BLK), jnp.float32)
        before = jnp.concatenate([first] + pieces[:-1], axis=0)
        parts = split3(jnp.concatenate([now, before], axis=1))
        n = now.shape[0]
        products = jnp.dot(jnp.concatenate(parts, axis=0), taps_ref[...], preferred_element_type=jnp.float32)
        filtered = jnp.zeros((n, BLK), jnp.float32)
        for total in (2, 1, 0):
            for i in range(total + 1):
                filtered = filtered + products[i * n : (i + 1) * n, (total - i) * BLK : (total - i + 1) * BLK]
        return filtered.astype(jnp.bfloat16).astype(jnp.float32)

    def scales_of(filtered):
        power = filtered * filtered
        high = power.astype(jnp.bfloat16)
        low = (power - high.astype(jnp.float32)).astype(jnp.bfloat16)
        taken = lax.broadcasted_iota(jnp.int32, (BLK, BLK), 0)
        at = lax.broadcasted_iota(jnp.int32, (BLK, BLK), 1)
        rest = jnp.where(taken >= at, 1.0, 0.0)
        masks = jnp.concatenate([rest, 1.0 - rest, jnp.ones((BLK, BLK), jnp.float32)], axis=1)
        sums = jnp.dot(
            jnp.concatenate([high, low], axis=0), masks.astype(jnp.bfloat16), preferred_element_type=jnp.float32
        )
        sums = sums[: power.shape[0]] + sums[power.shape[0] :]
        span = stations * time_blocks
        energy = sums[:span, :BLK] + sums[stations * lag_blocks :, BLK : 2 * BLK]
        for b in range(1, lag_blocks):
            energy = energy + sums[stations * b : stations * b + span, 2 * BLK :]
        inverse = 1.0 / jnp.sqrt(energy)
        return [
            [jnp.broadcast_to(inverse[stations * b + s : stations * b + s + 1], (ROWS, BLK)) for b in range(time_blocks)]
            for s in range(stations)
        ]

    tall = 16
    pairs = lag_blocks // 2
    time_pairs = time_blocks // 2

    def hankel(filtered, low, high, s):
        at = lax.broadcasted_iota(jnp.int32, (tall, BLK), 0) + lax.broadcasted_iota(jnp.int32, (tall, BLK), 1)
        lane = lax.broadcasted_iota(jnp.int32, (tall, BLK), 1)
        turned = [
            lane_gather(
                jnp.broadcast_to(filtered[stations * c + s : stations * c + s + 1, :], (tall, BLK)), at & (BLK - 1)
            )
            for c in range(high + 1 - low)
        ]
        heads = [
            jnp.where(at < BLK, turned[c], turned[min(c + 1, high - low)]).astype(jnp.bfloat16)
            for c in range(high + 1 - low)
        ]
        return {
            low + c: jnp.concatenate(
                [heads[c]]
                + [
                    pltpu.roll(jnp.where(lane < q, heads[c + 1], heads[c]), BLK - q, 1)
                    for q in range(tall, BLK, tall)
                ],
                axis=0,
            )
            for c in range(high - low)
        }

    def products(blocks, low, high, s, tops, add):
        raw = [None] * time_pairs
        if add:
            raw = [
                jnp.concatenate([raw_buf[s, p, top : top + 2 * ROWS] for top in tops], axis=0) for p in range(time_pairs)
            ]
        count = len(tops) * 2 * ROWS
        for c in range(low, high):
            tile = jnp.concatenate(
                [
                    jnp.concatenate([blocks[2 * c], blocks[2 * c + 1]], axis=1),
                    jnp.concatenate([blocks[2 * c + 1], blocks[2 * c + 2]], axis=1),
                ],
                axis=0,
            )
            used = [p for p in range(time_pairs) if 0 <= c - p < pairs]
            rows = jnp.concatenate(
                [tpl_split[s, pairs - 1 - (c - p), top : top + 2 * ROWS] for p in used for top in tops], axis=0
            )
            product = jnp.dot(rows, tile, preferred_element_type=jnp.float32)
            for i, p in enumerate(used):
                part = product[i * count : (i + 1) * count]
                raw[p] = part if raw[p] is None else raw[p] + part
        for p in range(time_pairs):
            for i, top in enumerate(tops):
                raw_buf[s, p, top : top + 2 * ROWS] = raw[p][i * 2 * ROWS : (i + 1) * 2 * ROWS]

    row_lane = lax.broadcasted_iota(jnp.int32, (ROWS, BLK), 1)

    def shift(top, scales):
        halves = []
        for at in (top, top + ROWS):
            stack = [None] * out_blocks
            for s in range(stations):
                moved = moved_ref[s, at : at + ROWS]
                weight = weight_ref[s, at : at + ROWS]
                index = (row_lane + moved) & (BLK - 1)
                stay = row_lane >= moved
                scaled = [
                    raw_buf[s, b // 2, at : at + ROWS, (b % 2) * BLK : (b % 2 + 1) * BLK] * scales[s][b]
                    for b in range(time_blocks)
                ]
                for b in range(out_blocks):
                    term = weight * lane_gather(jnp.where(stay, scaled[b], scaled[b + 1]), index)
                    stack[b] = term if stack[b] is None else stack[b] + term
            halves.append(jnp.concatenate(stack, axis=1))
        rows = jnp.concatenate(halves, axis=0).astype(jnp.bfloat16)
        send_buf[top // own_rows : (top + 2 * ROWS) // own_rows] = rows.reshape(
            2 * ROWS // own_rows, own_rows, out_blocks * BLK
        )

    def of_planes(planes):
        return [
            top
            for top in range(0, n_rows, 2 * ROWS)
            if any(
                owner % (dims[1] * dims[2]) // dims[2] in planes
                for owner in range(top // own_rows, (top + 2 * ROWS - 1) // own_rows + 1)
            )
        ]

    waves = [early[:2], early[2:], late]
    tops = [of_planes(planes) for planes in waves]
    tops[1] = [top for top in tops[1] if top not in tops[0]]
    tops[2] = [top for top in tops[2] if top not in tops[0] + tops[1]]

    def send(to):
        pltpu.make_async_remote_copy(
            src_ref=send_buf.at[to],
            dst_ref=recv_buf.at[me_s],
            send_sem=stack_send,
            recv_sem=stack_recv,
            device_id={"sta": to},
            device_id_type=MESH,
        ).start()

    def rest(low, before):
        start = 2 * low
        filtered = filter_blocks(0 if low == 0 else start + 2, wave_blocks)
        if low:
            filtered = jnp.concatenate([before, filtered], axis=0)
        scales = scales_of(filtered)
        blocks = []
        for s in range(stations):
            if low:
                blocks.append(hankel(filtered[stations * (start + 1) :], start + 1, wave_blocks - 1, s))
                blocks[s][start] = edge_buf[s]
            else:
                blocks.append(hankel(filtered, 0, wave_blocks - 1, s))
        for s in range(stations):
            products(blocks[s], low, pairs + time_pairs - 1, s, tops[0], low > 0)
        for s in range(stations):
            for b in range(time_blocks):
                scale_buf[s, b] = scales[s][b]
        for top in tops[0]:
            shift(top, scales)
        each(waves[0], send)
        for s in range(stations):
            products(blocks[s], low, pairs + time_pairs - 1, s, tops[1] + tops[2], low > 0)

    near_blocks = wave_blocks // 2
    near_pairs = (near_blocks - 2) // 2
    in_first = me_t < half
    wave_wait(0)

    @pl.when(in_first)
    def _():
        filtered = filter_blocks(0, near_blocks)
        filtered_buf[...] = filtered
        for s in range(stations):
            blocks = hankel(filtered, 0, near_blocks - 1, s)
            products(blocks, 0, near_pairs, s, sum(tops, []), False)
            edge_buf[s] = blocks[2 * near_pairs]

    wave_wait(1)
    wave_wait(2)

    @pl.when(in_first)
    def _():
        rest(near_pairs, filtered_buf[...])

    @pl.when(jnp.logical_not(in_first))
    def _():
        rest(0, None)

    scales = [[scale_buf[s, b] for b in range(time_blocks)] for s in range(stations)]
    for top in tops[1]:
        shift(top, scales)
    each(waves[1], send)
    for top in tops[2]:
        shift(top, scales)
    recv_buf[me_s] = send_buf[me_s]

    @pl.when(is_early)
    def _():
        pl.semaphore_wait(chain_sem.at[0], len(plane) * len(late))
        for at in late:
            @pl.when(me_z == nearest(at, early, dims[1]))
            def _():
                tell(chain_sem.at[1], place(0, 0, at))

    @pl.when(jnp.logical_not(is_early))
    def _():
        pl.semaphore_wait(chain_sem.at[1], 1)

    each(late, send)
    arrived = recv_buf.at[pl.ds(0, n_sta - 1)]
    pltpu.make_async_copy(arrived, arrived, stack_recv).wait()
    for copy in wave_copies:
        copy.wait_send()
    pltpu.make_async_copy(arrived, arrived, stack_send).wait()


def add_kernel(parts_ref, out_ref):
    out_ref[0] = jnp.sum(parts_ref[...].astype(jnp.float32), axis=0)


def shards(n_sta, n_tpl, waveform, fir_taps, templates, presence, moveout):
    stations, segment = waveform.shape
    n_rows, _, lags = templates.shape
    own_rows = n_rows // n_sta
    out_len = segment * n_tpl - lags - SHIFT_MOST
    lag_blocks = lags // BLK
    time_pairs = (segment * n_tpl // BLK - lag_blocks) // 2
    hbm = pl.BlockSpec(memory_space=pl.ANY)
    vmem = pl.BlockSpec(memory_space=pltpu.VMEM)
    parts = pl.pallas_call(
        functools.partial(kernel, n_sta, n_tpl),
        out_shape=pltpu.VMEM((n_sta, own_rows, out_len), jnp.bfloat16),
        in_specs=[hbm] * 5,
        out_specs=vmem,
        scratch_shapes=[
            pltpu.VMEM((n_tpl, stations, segment), jnp.float32),
            pltpu.VMEM((lag_blocks, n_rows, stations, BLK), jnp.bfloat16),
            pltpu.VMEM((2, n_rows * stations, BLK), jnp.float32),
            pltpu.VMEM((stations, lag_blocks // 2, n_rows, 2 * BLK), jnp.bfloat16),
            pltpu.VMEM((stations, time_pairs, n_rows, 2 * BLK), jnp.float32),
            pltpu.VMEM((stations * segment * n_tpl // (2 * BLK), BLK), jnp.float32),
            pltpu.VMEM((stations, BLK, BLK), jnp.bfloat16),
            pltpu.VMEM((stations, 2 * time_pairs, ROWS, BLK), jnp.float32),
            pltpu.VMEM((stations, n_rows, BLK), jnp.int32),
            pltpu.VMEM((stations, n_rows, BLK), jnp.float32),
            pltpu.VMEM((n_sta, own_rows, out_len), jnp.bfloat16),
            pltpu.VMEM((2 * BLK, 3 * BLK), jnp.bfloat16),
            pltpu.VMEM((1, fir_taps.shape[0]), jnp.float32),
            pltpu.VMEM((stations, n_rows), jnp.int32),
            pltpu.VMEM((stations, n_rows), jnp.int32),
            pltpu.SemaphoreType.DMA((1 + lag_blocks,)),
            pltpu.SemaphoreType.DMA((3,)),
            pltpu.SemaphoreType.REGULAR((2,)),
            pltpu.SemaphoreType.DMA((n_tpl - 1,)),
            pltpu.SemaphoreType.DMA((n_tpl - 1,)),
            pltpu.SemaphoreType.DMA,
            pltpu.SemaphoreType.DMA,
        ],
        compiler_params=pltpu.CompilerParams(
            collective_id=0, has_side_effects=True
        ),
    )(waveform, fir_taps[None, :], templates, presence.T, moveout.T)
    return pl.pallas_call(
        add_kernel,
        out_shape=jax.ShapeDtypeStruct((1, own_rows, out_len), jnp.float32),
        in_specs=[vmem],
        out_specs=vmem,
    )(pltpu.with_memory_space_constraint(parts, pltpu.VMEM))


def solution(mesh):
    placed = (P("sta", "tpl"), P(), P("tpl", "sta", None), P("tpl", "sta"), P("tpl", "sta"))
    return jax.shard_map(
        functools.partial(shards, mesh.shape["sta"], mesh.shape["tpl"]),
        mesh=mesh,
        in_specs=placed,
        out_specs=P("tpl", "sta", None),
        check_vma=False,
    )
```

```python
import functools

import jax
import jax.numpy as jnp
from jax import lax
from jax.experimental import pallas as pl
from jax.experimental.pallas import tpu as pltpu
from jax.sharding import PartitionSpec as P

BLK = 128
SHIFT_MOST = 128
ROWS = 8
EPSILON = 1e-06
MESH = pl.DeviceIdType.MESH


def lane_gather(values, index):
    return lax.gather(
        values,
        index[..., None],
        lax.GatherDimensionNumbers(
            offset_dims=(),
            collapsed_slice_dims=(1,),
            start_index_map=(1,),
            operand_batching_dims=(0,),
            start_indices_batching_dims=(0,),
        ),
        slice_sizes=(1, 1),
        mode=lax.GatherScatterMode.PROMISE_IN_BOUNDS,
    )


def split3(values):
    high = values.astype(jnp.bfloat16)
    rest = values - high.astype(jnp.float32)
    middle = rest.astype(jnp.bfloat16)
    low = (rest - middle.astype(jnp.float32)).astype(jnp.bfloat16)
    return [high, middle, low]


def sta_dims(n_sta):
    return {64: (2, 8, 4), 8: (2, 2, 2), 4: (2, 2, 1)}.get(n_sta, (1, n_sta, 1))


def places(me, dims):
    x, rest = me // (dims[1] * dims[2]), me % (dims[1] * dims[2])
    z, y = rest // dims[2], rest % dims[2]
    xs = [((x + d) % dims[0]) * (dims[1] * dims[2]) for d in range(dims[0])]
    ys = [(y + d) % dims[2] for d in range(dims[2])]
    return z, lambda dx, dy, at: xs[dx] + ys[dy] + at * dims[2]


def nearest(z, planes, n):
    return min(planes, key=lambda p: min((z - p) % n, (p - z) % n))


def kernel(
    n_sta,
    n_tpl,
    wave_ref,
    fir_hbm,
    tpl_ref,
    pres_hbm,
    mov_hbm,
    recv_buf,
    wave_buf,
    tpl_raw,
    rows32,
    tpl_split,
    raw_buf,
    filtered_buf,
    edge_buf,
    scale_buf,
    moved_ref,
    weight_ref,
    send_buf,
    taps_ref,
    fir_ref,
    pres_ref,
    mov_ref,
    local_sem,
    small_sem,
    chain_sem,
    wave_send,
    wave_recv,
    stack_send,
    stack_recv,
):
    me_s, me_t = lax.axis_index("sta"), lax.axis_index("tpl")
    dims = sta_dims(n_sta)
    me_z, place = places(me_s, dims)
    early = list(range(max(1, 3 * dims[1] // 8)))
    late = list(range(len(early), dims[1]))
    plane = [(dx, dy) for dx in range(dims[0]) for dy in range(dims[2])]
    plane.sort(key=lambda step: -sum(min(d, n - d) for d, n in zip(step, (dims[0], dims[2]))))
    is_early = me_z < len(early)
    stations = wave_ref.shape[0]
    n_rows = tpl_ref.shape[0]
    lag_blocks = tpl_ref.shape[2] // BLK
    own_rows = n_rows // n_sta
    seg_blocks = wave_ref.shape[1] // BLK
    wave_blocks = seg_blocks * n_tpl
    time_blocks = wave_blocks - lag_blocks
    out_blocks = time_blocks - 1

    def each(planes, do):
        for step in plane:
            for at in planes:
                to = place(*step, at)
                if step == (0, 0):
                    pl.when(me_z != at)(functools.partial(do, to))
                else:
                    do(to)

    def tell(sem, to):
        pl.semaphore_signal(sem, inc=1, device_id={"sta": to}, device_id_type=MESH)

    barrier = pltpu.get_barrier_semaphore()
    for step in range(n_tpl - 1, 0, -1):
        pl.semaphore_signal(barrier, inc=1, device_id={"tpl": lax.rem(me_t + step, n_tpl)}, device_id_type=MESH)

    @pl.when(is_early)
    def _():
        each(late + early, functools.partial(tell, barrier))

    own_wave = pltpu.make_async_copy(wave_ref, wave_buf.at[me_t], local_sem.at[0])
    own_wave.start()
    small_copies = [
        pltpu.make_async_copy(mov_hbm, mov_ref, small_sem.at[0]),
        pltpu.make_async_copy(pres_hbm, pres_ref, small_sem.at[1]),
        pltpu.make_async_copy(fir_hbm, fir_ref, small_sem.at[2]),
    ]
    for copy in small_copies:
        copy.start()
    tpl_copies = []
    for b in range(lag_blocks):
        tpl_copies.append(
            pltpu.make_async_copy(
                tpl_ref.at[:, :, pl.ds(b * BLK, BLK)], tpl_raw.at[b], local_sem.at[1 + b]
            )
        )
        tpl_copies[-1].start()

    n_early = len(plane) * len(early)
    pl.semaphore_wait(barrier, n_tpl - 1 + n_early - is_early.astype(jnp.int32))
    own_wave.wait()
    half = n_tpl // 2
    core = lax.rem(me_t, 2)
    across = lax.rem(me_t - core + half, n_tpl)
    wave_copies = [
        pltpu.make_async_remote_copy(
            src_ref=wave_buf.at[me_t],
            dst_ref=wave_buf.at[me_t],
            send_sem=wave_send.at[k],
            recv_sem=wave_recv.at[sem],
            device_id={"tpl": to},
            device_id_type=MESH,
        )
        for k, (to, sem) in enumerate(((across + 1, 1 + core), (across, 1 + core), (me_t + 1 - 2 * core, 0)))
    ]
    for copy in wave_copies:
        copy.start()

    def wave_wait(sem):
        pltpu.make_async_copy(wave_buf.at[0], wave_buf.at[0], wave_recv.at[sem]).wait()

    @pl.when(jnp.logical_not(is_early))
    def _():
        each(early, functools.partial(tell, chain_sem.at[0]))


    row_view = tpl_raw.reshape(lag_blocks, n_rows * stations, BLK)
    squares = [jnp.zeros((n_rows, BLK), jnp.float32) for _ in range(stations)]
    for b in range(lag_blocks):
        tpl_copies[b].wait()
        rows32[b % 2] = row_view[b].astype(jnp.float32)
        for s in range(stations):
            part = rows32[b % 2, pl.ds(s, n_rows, stride=stations), :]
            squares[s] = squares[s] + part * part
            tpl_split[s, lag_blocks // 2 - 1 - b // 2, :, (b % 2) * BLK : (b % 2 + 1) * BLK] = part.astype(
                jnp.bfloat16
            )

    for copy in small_copies:
        copy.wait()
    taps = jnp.concatenate([fir_ref[...], jnp.zeros((1, BLK - fir_ref.shape[1]), jnp.float32)], axis=1)
    from_at = lax.broadcasted_iota(jnp.int32, (BLK, BLK), 0)
    to_at = lax.broadcasted_iota(jnp.int32, (BLK, BLK), 1)
    turned = lane_gather(jnp.broadcast_to(taps, (BLK, BLK)), (to_at - from_at) & (BLK - 1))
    matrix = jnp.concatenate(
        [jnp.where(to_at >= from_at, turned, 0.0), jnp.where(to_at >= from_at, 0.0, turned)], axis=0
    )
    taps_ref[...] = jnp.concatenate(split3(matrix), axis=1)
    for s in range(stations):
        norm = jnp.sqrt(jnp.sum(squares[s], axis=1, keepdims=True) + EPSILON)
        moved = jnp.transpose(jnp.broadcast_to(mov_ref[s : s + 1, :], (BLK, n_rows)))
        present = jnp.transpose(jnp.broadcast_to(pres_ref[s : s + 1, :].astype(jnp.float32), (BLK, n_rows)))
        weight_ref[s] = present / norm
        moved_ref[s] = moved

    def piece(c):
        return wave_buf[c // seg_blocks, :, (c % seg_blocks) * BLK : (c % seg_blocks + 1) * BLK]

    def filter_blocks(low, high):
        pieces = [piece(c) for c in range(low, high)]
        now = jnp.concatenate(pieces, axis=0)
        first = piece(low - 1) if low else jnp.zeros((stations, BLK), jnp.float32)
        before = jnp.concatenate([first] + pieces[:-1], axis=0)
        parts = split3(jnp.concatenate([now, before], axis=1))
        n = now.shape[0]
        products = jnp.dot(jnp.concatenate(parts, axis=0), taps_ref[...], preferred_element_type=jnp.float32)
        filtered = jnp.zeros((n, BLK), jnp.float32)
        for total in (2, 1, 0):
            for i in range(total + 1):
                filtered = filtered + products[i * n : (i + 1) * n, (total - i) * BLK : (total - i + 1) * BLK]
        return filtered.astype(jnp.bfloat16).astype(jnp.float32)

    def scales_of(filtered):
        power = filtered * filtered
        high = power.astype(jnp.bfloat16)
        low = (power - high.astype(jnp.float32)).astype(jnp.bfloat16)
        taken = lax.broadcasted_iota(jnp.int32, (BLK, BLK), 0)
        at = lax.broadcasted_iota(jnp.int32, (BLK, BLK), 1)
        rest = jnp.where(taken >= at, 1.0, 0.0)
        masks = jnp.concatenate([rest, 1.0 - rest, jnp.ones((BLK, BLK), jnp.float32)], axis=1)
        sums = jnp.dot(
            jnp.concatenate([high, low], axis=0), masks.astype(jnp.bfloat16), preferred_element_type=jnp.float32
        )
        sums = sums[: power.shape[0]] + sums[power.shape[0] :]
        span = stations * time_blocks
        energy = sums[:span, :BLK] + sums[stations * lag_blocks :, BLK : 2 * BLK]
        for b in range(1, lag_blocks):
            energy = energy + sums[stations * b : stations * b + span, 2 * BLK :]
        inverse = 1.0 / jnp.sqrt(energy)
        return [
            [jnp.broadcast_to(inverse[stations * b + s : stations * b + s + 1], (ROWS, BLK)) for b in range(time_blocks)]
            for s in range(stations)
        ]

    tall = 16
    pairs = lag_blocks // 2
    time_pairs = time_blocks // 2

    def hankel(filtered, low, high, s):
        at = lax.broadcasted_iota(jnp.int32, (tall, BLK), 0) + lax.broadcasted_iota(jnp.int32, (tall, BLK), 1)
        lane = lax.broadcasted_iota(jnp.int32, (tall, BLK), 1)
        turned = [
            lane_gather(
                jnp.broadcast_to(filtered[stations * c + s : stations * c + s + 1, :], (tall, BLK)), at & (BLK - 1)
            )
            for c in range(high + 1 - low)
        ]
        heads = [
            jnp.where(at < BLK, turned[c], turned[min(c + 1, high - low)]).astype(jnp.bfloat16)
            for c in range(high + 1 - low)
        ]
        return {
            low + c: jnp.concatenate(
                [heads[c]]
                + [
                    pltpu.roll(jnp.where(lane < q, heads[c + 1], heads[c]), BLK - q, 1)
                    for q in range(tall, BLK, tall)
                ],
                axis=0,
            )
            for c in range(high - low)
        }

    def products(blocks, low, high, s, tops, add):
        raw = [None] * time_pairs
        if add:
            raw = [
                jnp.concatenate([raw_buf[s, p, top : top + 2 * ROWS] for top in tops], axis=0) for p in range(time_pairs)
            ]
        count = len(tops) * 2 * ROWS
        for c in range(low, high):
            tile = jnp.concatenate(
                [
                    jnp.concatenate([blocks[2 * c], blocks[2 * c + 1]], axis=1),
                    jnp.concatenate([blocks[2 * c + 1], blocks[2 * c + 2]], axis=1),
                ],
                axis=0,
            )
            used = [p for p in range(time_pairs) if 0 <= c - p < pairs]
            rows = jnp.concatenate(
                [tpl_split[s, pairs - 1 - (c - p), top : top + 2 * ROWS] for p in used for top in tops], axis=0
            )
            product = jnp.dot(rows, tile, preferred_element_type=jnp.float32)
            for i, p in enumerate(used):
                part = product[i * count : (i + 1) * count]
                raw[p] = part if raw[p] is None else raw[p] + part
        for p in range(time_pairs):
            for i, top in enumerate(tops):
                raw_buf[s, p, top : top + 2 * ROWS] = raw[p][i * 2 * ROWS : (i + 1) * 2 * ROWS]

    row_lane = lax.broadcasted_iota(jnp.int32, (ROWS, BLK), 1)

    def shift(top, scales):
        halves = []
        for at in (top, top + ROWS):
            stack = [None] * out_blocks
            for s in range(stations):
                moved = moved_ref[s, at : at + ROWS]
                weight = weight_ref[s, at : at + ROWS]
                index = (row_lane + moved) & (BLK - 1)
                stay = row_lane >= moved
                scaled = [
                    raw_buf[s, b // 2, at : at + ROWS, (b % 2) * BLK : (b % 2 + 1) * BLK] * scales[s][b]
                    for b in range(time_blocks)
                ]
                for b in range(out_blocks):
                    term = weight * lane_gather(jnp.where(stay, scaled[b], scaled[b + 1]), index)
                    stack[b] = term if stack[b] is None else stack[b] + term
            halves.append(jnp.concatenate(stack, axis=1))
        rows = jnp.concatenate(halves, axis=0).astype(jnp.bfloat16)
        send_buf[top // own_rows : (top + 2 * ROWS) // own_rows] = rows.reshape(
            2 * ROWS // own_rows, own_rows, out_blocks * BLK
        )

    def of_planes(planes):
        return [
            top
            for top in range(0, n_rows, 2 * ROWS)
            if any(
                owner % (dims[1] * dims[2]) // dims[2] in planes
                for owner in range(top // own_rows, (top + 2 * ROWS - 1) // own_rows + 1)
            )
        ]

    waves = [early[:2], early[2:], late]
    tops = [of_planes(planes) for planes in waves]
    tops[1] = [top for top in tops[1] if top not in tops[0]]
    tops[2] = [top for top in tops[2] if top not in tops[0] + tops[1]]

    def send(to):
        pltpu.make_async_remote_copy(
            src_ref=send_buf.at[to],
            dst_ref=recv_buf.at[me_s],
            send_sem=stack_send,
            recv_sem=stack_recv,
            device_id={"sta": to},
            device_id_type=MESH,
        ).start()

    def rest(low, before):
        start = 2 * low
        filtered = filter_blocks(0 if low == 0 else start + 2, wave_blocks)
        if low:
            filtered = jnp.concatenate([before, filtered], axis=0)
        scales = scales_of(filtered)
        blocks = []
        for s in range(stations):
            if low:
                blocks.append(hankel(filtered[stations * (start + 1) :], start + 1, wave_blocks - 1, s))
                blocks[s][start] = edge_buf[s]
            else:
                blocks.append(hankel(filtered, 0, wave_blocks - 1, s))
            products(blocks[s], low, pairs + time_pairs - 1, s, tops[0], low > 0)
        for s in range(stations):
            for b in range(time_blocks):
                scale_buf[s, b] = scales[s][b]
        for top in tops[0]:
            shift(top, scales)
        each(waves[0], send)
        for s in range(stations):
            products(blocks[s], low, pairs + time_pairs - 1, s, tops[1] + tops[2], low > 0)

    near_blocks = wave_blocks // 2
    near_pairs = (near_blocks - 2) // 2
    in_first = me_t < half
    wave_wait(0)

    @pl.when(in_first)
    def _():
        filtered = filter_blocks(0, near_blocks)
        filtered_buf[...] = filtered
        for s in range(stations):
            blocks = hankel(filtered, 0, near_blocks - 1, s)
            products(blocks, 0, near_pairs, s, sum(tops, []), False)
            edge_buf[s] = blocks[2 * near_pairs]

    wave_wait(1)
    wave_wait(2)

    @pl.when(in_first)
    def _():
        rest(near_pairs, filtered_buf[...])

    @pl.when(jnp.logical_not(in_first))
    def _():
        rest(0, None)

    scales = [[scale_buf[s, b] for b in range(time_blocks)] for s in range(stations)]
    for top in tops[1]:
        shift(top, scales)
    each(waves[1], send)
    for top in tops[2]:
        shift(top, scales)
    recv_buf[me_s] = send_buf[me_s]

    @pl.when(is_early)
    def _():
        pl.semaphore_wait(chain_sem.at[0], len(plane) * len(late))
        for at in late:
            @pl.when(me_z == nearest(at, early, dims[1]))
            def _():
                tell(chain_sem.at[1], place(0, 0, at))

    @pl.when(jnp.logical_not(is_early))
    def _():
        pl.semaphore_wait(chain_sem.at[1], 1)

    each(late, send)
    arrived = recv_buf.at[pl.ds(0, n_sta - 1)]
    pltpu.make_async_copy(arrived, arrived, stack_recv).wait()
    for copy in wave_copies:
        copy.wait_send()
    pltpu.make_async_copy(arrived, arrived, stack_send).wait()


def shards(n_sta, n_tpl, waveform, fir_taps, templates, presence, moveout):
    stations, segment = waveform.shape
    n_rows, _, lags = templates.shape
    own_rows = n_rows // n_sta
    out_len = segment * n_tpl - lags - SHIFT_MOST
    lag_blocks = lags // BLK
    time_pairs = (segment * n_tpl // BLK - lag_blocks) // 2
    hbm = pl.BlockSpec(memory_space=pl.ANY)
    vmem = pl.BlockSpec(memory_space=pltpu.VMEM)
    parts = pl.pallas_call(
        functools.partial(kernel, n_sta, n_tpl),
        out_shape=pltpu.VMEM((n_sta, own_rows, out_len), jnp.bfloat16),
        in_specs=[hbm] * 5,
        out_specs=vmem,
        scratch_shapes=[
            pltpu.VMEM((n_tpl, stations, segment), jnp.float32),
            pltpu.VMEM((lag_blocks, n_rows, stations, BLK), jnp.bfloat16),
            pltpu.VMEM((2, n_rows * stations, BLK), jnp.float32),
            pltpu.VMEM((stations, lag_blocks // 2, n_rows, 2 * BLK), jnp.bfloat16),
            pltpu.VMEM((stations, time_pairs, n_rows, 2 * BLK), jnp.float32),
            pltpu.VMEM((stations * segment * n_tpl // (2 * BLK), BLK), jnp.float32),
            pltpu.VMEM((stations, BLK, BLK), jnp.bfloat16),
            pltpu.VMEM((stations, 2 * time_pairs, ROWS, BLK), jnp.float32),
            pltpu.VMEM((stations, n_rows, BLK), jnp.int32),
            pltpu.VMEM((stations, n_rows, BLK), jnp.float32),
            pltpu.VMEM((n_sta, own_rows, out_len), jnp.bfloat16),
            pltpu.VMEM((2 * BLK, 3 * BLK), jnp.bfloat16),
            pltpu.VMEM((1, fir_taps.shape[0]), jnp.float32),
            pltpu.VMEM((stations, n_rows), jnp.int32),
            pltpu.VMEM((stations, n_rows), jnp.int32),
            pltpu.SemaphoreType.DMA((1 + lag_blocks,)),
            pltpu.SemaphoreType.DMA((3,)),
            pltpu.SemaphoreType.REGULAR((2,)),
            pltpu.SemaphoreType.DMA((n_tpl - 1,)),
            pltpu.SemaphoreType.DMA((n_tpl - 1,)),
            pltpu.SemaphoreType.DMA,
            pltpu.SemaphoreType.DMA,
        ],
        compiler_params=pltpu.CompilerParams(
            collective_id=0, has_side_effects=True
        ),
    )(waveform, fir_taps[None, :], templates, presence.T, moveout.T)
    return jnp.sum(parts.astype(jnp.float32), axis=0)[None]


def solution(mesh):
    placed = (P("sta", "tpl"), P(), P("tpl", "sta", None), P("tpl", "sta"), P("tpl", "sta"))
    return jax.shard_map(
        functools.partial(shards, mesh.shape["sta"], mesh.shape["tpl"]),
        mesh=mesh,
        in_specs=placed,
        out_specs=P("tpl", "sta", None),
        check_vma=False,
    )
```

```python
import functools

import jax
import jax.numpy as jnp
from jax import lax
from jax.experimental import pallas as pl
from jax.experimental.pallas import tpu as pltpu
from jax.sharding import PartitionSpec as P

BLK = 128
SHIFT_MOST = 128
ROWS = 8
EPSILON = 1e-06
MESH = pl.DeviceIdType.MESH


def lane_gather(values, index):
    return lax.gather(
        values,
        index[..., None],
        lax.GatherDimensionNumbers(
            offset_dims=(),
            collapsed_slice_dims=(1,),
            start_index_map=(1,),
            operand_batching_dims=(0,),
            start_indices_batching_dims=(0,),
        ),
        slice_sizes=(1, 1),
        mode=lax.GatherScatterMode.PROMISE_IN_BOUNDS,
    )


def split3(values):
    high = values.astype(jnp.bfloat16)
    rest = values - high.astype(jnp.float32)
    middle = rest.astype(jnp.bfloat16)
    low = (rest - middle.astype(jnp.float32)).astype(jnp.bfloat16)
    return [high, middle, low]


def sta_dims(n_sta):
    return {64: (2, 8, 4), 8: (2, 2, 2), 4: (2, 2, 1)}.get(n_sta, (1, n_sta, 1))


def places(me, dims):
    x, rest = me // (dims[1] * dims[2]), me % (dims[1] * dims[2])
    z, y = rest // dims[2], rest % dims[2]
    xs = [((x + d) % dims[0]) * (dims[1] * dims[2]) for d in range(dims[0])]
    ys = [(y + d) % dims[2] for d in range(dims[2])]
    return z, lambda dx, dy, at: xs[dx] + ys[dy] + at * dims[2]


def nearest(z, planes, n):
    return min(planes, key=lambda p: min((z - p) % n, (p - z) % n))


def kernel(
    n_sta,
    n_tpl,
    wave_ref,
    fir_hbm,
    tpl_ref,
    pres_hbm,
    mov_hbm,
    recv_buf,
    wave_buf,
    tpl_raw,
    rows32,
    tpl_split,
    raw_buf,
    filtered_buf,
    edge_buf,
    scale_buf,
    moved_ref,
    weight_ref,
    send_buf,
    taps_ref,
    fir_ref,
    pres_ref,
    mov_ref,
    local_sem,
    small_sem,
    chain_sem,
    wave_send,
    wave_recv,
    stack_send,
    stack_recv,
):
    me_s, me_t = lax.axis_index("sta"), lax.axis_index("tpl")
    dims = sta_dims(n_sta)
    me_z, place = places(me_s, dims)
    early = list(range(max(1, 3 * dims[1] // 8)))
    late = list(range(len(early), dims[1]))
    plane = [(dx, dy) for dx in range(dims[0]) for dy in range(dims[2])]
    plane.sort(key=lambda step: -sum(min(d, n - d) for d, n in zip(step, (dims[0], dims[2]))))
    is_early = me_z < len(early)
    stations = wave_ref.shape[0]
    n_rows = tpl_ref.shape[0]
    lag_blocks = tpl_ref.shape[2] // BLK
    own_rows = n_rows // n_sta
    seg_blocks = wave_ref.shape[1] // BLK
    wave_blocks = seg_blocks * n_tpl
    time_blocks = wave_blocks - lag_blocks
    out_blocks = time_blocks - 1

    def each(planes, do):
        for step in plane:
            for at in planes:
                to = place(*step, at)
                if step == (0, 0):
                    pl.when(me_z != at)(functools.partial(do, to))
                else:
                    do(to)

    def tell(sem, to):
        pl.semaphore_signal(sem, inc=1, device_id={"sta": to}, device_id_type=MESH)

    barrier = pltpu.get_barrier_semaphore()
    for step in range(n_tpl - 1, 0, -1):
        pl.semaphore_signal(barrier, inc=1, device_id={"tpl": lax.rem(me_t + step, n_tpl)}, device_id_type=MESH)

    @pl.when(is_early)
    def _():
        each(late + early, functools.partial(tell, barrier))

    own_wave = pltpu.make_async_copy(wave_ref, wave_buf.at[me_t], local_sem.at[0])
    own_wave.start()
    small_copies = [
        pltpu.make_async_copy(mov_hbm, mov_ref, small_sem.at[0]),
        pltpu.make_async_copy(pres_hbm, pres_ref, small_sem.at[1]),
        pltpu.make_async_copy(fir_hbm, fir_ref, small_sem.at[2]),
    ]
    for copy in small_copies:
        copy.start()
    tpl_copies = []
    for b in range(lag_blocks):
        tpl_copies.append(
            pltpu.make_async_copy(
                tpl_ref.at[:, :, pl.ds(b * BLK, BLK)], tpl_raw.at[b], local_sem.at[1 + b]
            )
        )
        tpl_copies[-1].start()

    n_early = len(plane) * len(early)
    pl.semaphore_wait(barrier, n_tpl - 1 + n_early - is_early.astype(jnp.int32))
    own_wave.wait()
    half = n_tpl // 2
    core = lax.rem(me_t, 2)
    across = lax.rem(me_t - core + half, n_tpl)
    wave_copies = [
        pltpu.make_async_remote_copy(
            src_ref=wave_buf.at[me_t],
            dst_ref=wave_buf.at[me_t],
            send_sem=wave_send.at[k],
            recv_sem=wave_recv.at[sem],
            device_id={"tpl": to},
            device_id_type=MESH,
        )
        for k, (to, sem) in enumerate(((across + 1, 1 + core), (across, 1 + core), (me_t + 1 - 2 * core, 0)))
    ]
    for copy in wave_copies:
        copy.start()

    def wave_wait(sem):
        pltpu.make_async_copy(wave_buf.at[0], wave_buf.at[0], wave_recv.at[sem]).wait()

    @pl.when(jnp.logical_not(is_early))
    def _():
        each(early, functools.partial(tell, chain_sem.at[0]))


    row_view = tpl_raw.reshape(lag_blocks, n_rows * stations, BLK)
    squares = [jnp.zeros((n_rows, BLK), jnp.float32) for _ in range(stations)]
    for b in range(lag_blocks):
        tpl_copies[b].wait()
        rows32[b % 2] = row_view[b].astype(jnp.float32)
        for s in range(stations):
            part = rows32[b % 2, pl.ds(s, n_rows, stride=stations), :]
            squares[s] = squares[s] + part * part
            tpl_split[s, lag_blocks // 2 - 1 - b // 2, :, (b % 2) * BLK : (b % 2 + 1) * BLK] = part.astype(
                jnp.bfloat16
            )

    for copy in small_copies:
        copy.wait()
    taps = jnp.concatenate([fir_ref[...], jnp.zeros((1, BLK - fir_ref.shape[1]), jnp.float32)], axis=1)
    from_at = lax.broadcasted_iota(jnp.int32, (BLK, BLK), 0)
    to_at = lax.broadcasted_iota(jnp.int32, (BLK, BLK), 1)
    turned = lane_gather(jnp.broadcast_to(taps, (BLK, BLK)), (to_at - from_at) & (BLK - 1))
    matrix = jnp.concatenate(
        [jnp.where(to_at >= from_at, turned, 0.0), jnp.where(to_at >= from_at, 0.0, turned)], axis=0
    )
    taps_ref[...] = jnp.concatenate(split3(matrix), axis=1)
    for s in range(stations):
        norm = jnp.sqrt(jnp.sum(squares[s], axis=1, keepdims=True) + EPSILON)
        moved = jnp.transpose(jnp.broadcast_to(mov_ref[s : s + 1, :], (BLK, n_rows)))
        present = jnp.transpose(jnp.broadcast_to(pres_ref[s : s + 1, :].astype(jnp.float32), (BLK, n_rows)))
        weight_ref[s] = present / norm
        moved_ref[s] = moved

    def piece(c):
        return wave_buf[c // seg_blocks, :, (c % seg_blocks) * BLK : (c % seg_blocks + 1) * BLK]

    def filter_blocks(low, high):
        pieces = [piece(c) for c in range(low, high)]
        now = jnp.concatenate(pieces, axis=0)
        first = piece(low - 1) if low else jnp.zeros((stations, BLK), jnp.float32)
        before = jnp.concatenate([first] + pieces[:-1], axis=0)
        parts = split3(jnp.concatenate([now, before], axis=1))
        n = now.shape[0]
        products = jnp.dot(jnp.concatenate(parts, axis=0), taps_ref[...], preferred_element_type=jnp.float32)
        filtered = jnp.zeros((n, BLK), jnp.float32)
        for total in (2, 1, 0):
            for i in range(total + 1):
                filtered = filtered + products[i * n : (i + 1) * n, (total - i) * BLK : (total - i + 1) * BLK]
        return filtered.astype(jnp.bfloat16).astype(jnp.float32)

    def scales_of(filtered):
        power = filtered * filtered
        high = power.astype(jnp.bfloat16)
        low = (power - high.astype(jnp.float32)).astype(jnp.bfloat16)
        taken = lax.broadcasted_iota(jnp.int32, (BLK, BLK), 0)
        at = lax.broadcasted_iota(jnp.int32, (BLK, BLK), 1)
        rest = jnp.where(taken >= at, 1.0, 0.0)
        masks = jnp.concatenate([rest, 1.0 - rest, jnp.ones((BLK, BLK), jnp.float32)], axis=1)
        sums = jnp.dot(
            jnp.concatenate([high, low], axis=0), masks.astype(jnp.bfloat16), preferred_element_type=jnp.float32
        )
        sums = sums[: power.shape[0]] + sums[power.shape[0] :]
        span = stations * time_blocks
        energy = sums[:span, :BLK] + sums[stations * lag_blocks :, BLK : 2 * BLK]
        for b in range(1, lag_blocks):
            energy = energy + sums[stations * b : stations * b + span, 2 * BLK :]
        inverse = 1.0 / jnp.sqrt(energy)
        return [
            [jnp.broadcast_to(inverse[stations * b + s : stations * b + s + 1], (ROWS, BLK)) for b in range(time_blocks)]
            for s in range(stations)
        ]

    tall = 16
    pairs = lag_blocks // 2
    time_pairs = time_blocks // 2

    def hankel(filtered, low, high, s):
        at = lax.broadcasted_iota(jnp.int32, (tall, BLK), 0) + lax.broadcasted_iota(jnp.int32, (tall, BLK), 1)
        lane = lax.broadcasted_iota(jnp.int32, (tall, BLK), 1)
        turned = [
            lane_gather(
                jnp.broadcast_to(filtered[stations * c + s : stations * c + s + 1, :], (tall, BLK)), at & (BLK - 1)
            )
            for c in range(high + 1 - low)
        ]
        heads = [
            jnp.where(at < BLK, turned[c], turned[min(c + 1, high - low)]).astype(jnp.bfloat16)
            for c in range(high + 1 - low)
        ]
        return {
            low + c: jnp.concatenate(
                [heads[c]]
                + [
                    pltpu.roll(jnp.where(lane < q, heads[c + 1], heads[c]), BLK - q, 1)
                    for q in range(tall, BLK, tall)
                ],
                axis=0,
            )
            for c in range(high - low)
        }

    def products(blocks, low, high, s, tops, add):
        raw = [None] * time_pairs
        if add:
            raw = [
                jnp.concatenate([raw_buf[s, p, top : top + 2 * ROWS] for top in tops], axis=0) for p in range(time_pairs)
            ]
        count = len(tops) * 2 * ROWS
        for c in range(low, high):
            tile = jnp.concatenate(
                [
                    jnp.concatenate([blocks[2 * c], blocks[2 * c + 1]], axis=1),
                    jnp.concatenate([blocks[2 * c + 1], blocks[2 * c + 2]], axis=1),
                ],
                axis=0,
            )
            used = [p for p in range(time_pairs) if 0 <= c - p < pairs]
            rows = jnp.concatenate(
                [tpl_split[s, pairs - 1 - (c - p), top : top + 2 * ROWS] for p in used for top in tops], axis=0
            )
            product = jnp.dot(rows, tile, preferred_element_type=jnp.float32)
            for i, p in enumerate(used):
                part = product[i * count : (i + 1) * count]
                raw[p] = part if raw[p] is None else raw[p] + part
        for p in range(time_pairs):
            for i, top in enumerate(tops):
                raw_buf[s, p, top : top + 2 * ROWS] = raw[p][i * 2 * ROWS : (i + 1) * 2 * ROWS]

    row_lane = lax.broadcasted_iota(jnp.int32, (ROWS, BLK), 1)

    def shift(top, scales):
        halves = []
        for at in (top, top + ROWS):
            stack = [None] * out_blocks
            for s in range(stations):
                moved = moved_ref[s, at : at + ROWS]
                weight = weight_ref[s, at : at + ROWS]
                index = (row_lane + moved) & (BLK - 1)
                stay = row_lane >= moved
                scaled = [
                    raw_buf[s, b // 2, at : at + ROWS, (b % 2) * BLK : (b % 2 + 1) * BLK] * scales[s][b]
                    for b in range(time_blocks)
                ]
                for b in range(out_blocks):
                    term = weight * lane_gather(jnp.where(stay, scaled[b], scaled[b + 1]), index)
                    stack[b] = term if stack[b] is None else stack[b] + term
            halves.append(jnp.concatenate(stack, axis=1))
        rows = jnp.concatenate(halves, axis=0).astype(jnp.bfloat16)
        send_buf[top // own_rows : (top + 2 * ROWS) // own_rows] = rows.reshape(
            2 * ROWS // own_rows, own_rows, out_blocks * BLK
        )

    def of_planes(planes):
        return [
            top
            for top in range(0, n_rows, 2 * ROWS)
            if any(
                owner % (dims[1] * dims[2]) // dims[2] in planes
                for owner in range(top // own_rows, (top + 2 * ROWS - 1) // own_rows + 1)
            )
        ]

    waves = [early[:2], early[2:], late]
    tops = [of_planes(planes) for planes in waves]
    tops[1] = [top for top in tops[1] if top not in tops[0]]
    tops[2] = [top for top in tops[2] if top not in tops[0] + tops[1]]

    def send(to):
        pltpu.make_async_remote_copy(
            src_ref=send_buf.at[to],
            dst_ref=recv_buf.at[me_s],
            send_sem=stack_send,
            recv_sem=stack_recv,
            device_id={"sta": to},
            device_id_type=MESH,
        ).start()

    def rest(low, before):
        start = 2 * low
        filtered = filter_blocks(0 if low == 0 else start + 2, wave_blocks)
        if low:
            filtered = jnp.concatenate([before, filtered], axis=0)
        blocks = []
        for s in range(stations):
            if low:
                blocks.append(hankel(filtered[stations * (start + 1) :], start + 1, wave_blocks - 1, s))
                blocks[s][start] = edge_buf[s]
            else:
                blocks.append(hankel(filtered, 0, wave_blocks - 1, s))
        for s in range(stations):
            products(blocks[s], low, pairs + time_pairs - 1, s, tops[0], low > 0)
        scales = scales_of(filtered)
        for s in range(stations):
            for b in range(time_blocks):
                scale_buf[s, b] = scales[s][b]
        for top in tops[0]:
            shift(top, scales)
        each(waves[0], send)
        for s in range(stations):
            products(blocks[s], low, pairs + time_pairs - 1, s, tops[1] + tops[2], low > 0)

    near_blocks = wave_blocks // 2
    near_pairs = (near_blocks - 2) // 2
    in_first = me_t < half
    wave_wait(0)

    @pl.when(in_first)
    def _():
        filtered = filter_blocks(0, near_blocks)
        filtered_buf[...] = filtered
        for s in range(stations):
            blocks = hankel(filtered, 0, near_blocks - 1, s)
            products(blocks, 0, near_pairs, s, sum(tops, []), False)
            edge_buf[s] = blocks[2 * near_pairs]

    wave_wait(1)
    wave_wait(2)

    @pl.when(in_first)
    def _():
        rest(near_pairs, filtered_buf[...])

    @pl.when(jnp.logical_not(in_first))
    def _():
        rest(0, None)

    scales = [[scale_buf[s, b] for b in range(time_blocks)] for s in range(stations)]
    for top in tops[1]:
        shift(top, scales)
    each(waves[1], send)
    for top in tops[2]:
        shift(top, scales)
    recv_buf[me_s] = send_buf[me_s]

    @pl.when(is_early)
    def _():
        pl.semaphore_wait(chain_sem.at[0], len(plane) * len(late))
        for at in late:
            @pl.when(me_z == nearest(at, early, dims[1]))
            def _():
                tell(chain_sem.at[1], place(0, 0, at))

    @pl.when(jnp.logical_not(is_early))
    def _():
        pl.semaphore_wait(chain_sem.at[1], 1)

    each(late, send)
    arrived = recv_buf.at[pl.ds(0, n_sta - 1)]
    pltpu.make_async_copy(arrived, arrived, stack_recv).wait()
    for copy in wave_copies:
        copy.wait_send()
    pltpu.make_async_copy(arrived, arrived, stack_send).wait()


def add_kernel(parts_ref, out_ref):
    out_ref[0] = jnp.sum(parts_ref[...].astype(jnp.float32), axis=0)


def shards(n_sta, n_tpl, waveform, fir_taps, templates, presence, moveout):
    stations, segment = waveform.shape
    n_rows, _, lags = templates.shape
    own_rows = n_rows // n_sta
    out_len = segment * n_tpl - lags - SHIFT_MOST
    lag_blocks = lags // BLK
    time_pairs = (segment * n_tpl // BLK - lag_blocks) // 2
    hbm = pl.BlockSpec(memory_space=pl.ANY)
    vmem = pl.BlockSpec(memory_space=pltpu.VMEM)
    parts = pl.pallas_call(
        functools.partial(kernel, n_sta, n_tpl),
        out_shape=pltpu.VMEM((n_sta, own_rows, out_len), jnp.bfloat16),
        in_specs=[hbm] * 5,
        out_specs=vmem,
        scratch_shapes=[
            pltpu.VMEM((n_tpl, stations, segment), jnp.float32),
            pltpu.VMEM((lag_blocks, n_rows, stations, BLK), jnp.bfloat16),
            pltpu.VMEM((2, n_rows * stations, BLK), jnp.float32),
            pltpu.VMEM((stations, lag_blocks // 2, n_rows, 2 * BLK), jnp.bfloat16),
            pltpu.VMEM((stations, time_pairs, n_rows, 2 * BLK), jnp.float32),
            pltpu.VMEM((stations * segment * n_tpl // (2 * BLK), BLK), jnp.float32),
            pltpu.VMEM((stations, BLK, BLK), jnp.bfloat16),
            pltpu.VMEM((stations, 2 * time_pairs, ROWS, BLK), jnp.float32),
            pltpu.VMEM((stations, n_rows, BLK), jnp.int32),
            pltpu.VMEM((stations, n_rows, BLK), jnp.float32),
            pltpu.VMEM((n_sta, own_rows, out_len), jnp.bfloat16),
            pltpu.VMEM((2 * BLK, 3 * BLK), jnp.bfloat16),
            pltpu.VMEM((1, fir_taps.shape[0]), jnp.float32),
            pltpu.VMEM((stations, n_rows), jnp.int32),
            pltpu.VMEM((stations, n_rows), jnp.int32),
            pltpu.SemaphoreType.DMA((1 + lag_blocks,)),
            pltpu.SemaphoreType.DMA((3,)),
            pltpu.SemaphoreType.REGULAR((2,)),
            pltpu.SemaphoreType.DMA((n_tpl - 1,)),
            pltpu.SemaphoreType.DMA((n_tpl - 1,)),
            pltpu.SemaphoreType.DMA,
            pltpu.SemaphoreType.DMA,
        ],
        compiler_params=pltpu.CompilerParams(
            collective_id=0, has_side_effects=True
        ),
    )(waveform, fir_taps[None, :], templates, presence.T, moveout.T)
    return pl.pallas_call(
        add_kernel,
        out_shape=jax.ShapeDtypeStruct((1, own_rows, out_len), jnp.float32),
        in_specs=[vmem],
        out_specs=vmem,
    )(pltpu.with_memory_space_constraint(parts, pltpu.VMEM))


def solution(mesh):
    placed = (P("sta", "tpl"), P(), P("tpl", "sta", None), P("tpl", "sta"), P("tpl", "sta"))
    return jax.shard_map(
        functools.partial(shards, mesh.shape["sta"], mesh.shape["tpl"]),
        mesh=mesh,
        in_specs=placed,
        out_specs=P("tpl", "sta", None),
        check_vma=False,
    )
```
